32 devices in a mesh: rep: 4 (over y, x), fsdp: 2 (over core), tp: 4 (over z).
Axes of the slice: x: 2, y: 2, z: 4, core: 2. Of those that a mesh axis runs over, the one named last changes fastest.
Arguments:
- grad_parts: bfloat16 [2, 2, 8192, 1024], P('fsdp', None, 'rep', 'tp'), may hold values from -4 to 4
- master_weight: float32 [2, 8192, 1024], P(None, ('rep', 'fsdp'), 'tp'), may hold values from -0.0625 to 0.0625
- moment_one: float32 [2, 8192, 1024], P(None, ('rep', 'fsdp'), 'tp'), may hold values from -4 to 4
- moment_two: float32 [2, 8192, 1024], P(None, ('rep', 'fsdp'), 'tp'), may hold values from 0.1 to 2
- layer_inputs: bfloat16 [384, 4, 8192], P(('rep', 'fsdp'), None, 'tp'), may hold values from -6 to 6
- queries: bfloat16 [384, 4, 8192], P(('rep', 'fsdp'), None, 'tp'), may hold values from -105 to 105
- kv_cache: bfloat16 [384, 24, 2, 1024], P(('rep', 'fsdp'), None, None, 'tp'), may hold values from -4 to 4
- lengths: int32 [384], P(('rep', 'fsdp')), may hold values from 2 to 24
Outputs:
- new_master: float32 [2, 8192, 1024], P(None, ('rep', 'fsdp'), 'tp')
- new_moment_one: float32 [2, 8192, 1024], P(None, ('rep', 'fsdp'), 'tp')
- new_moment_two: float32 [2, 8192, 1024], P(None, ('rep', 'fsdp'), 'tp')
- context: bfloat16 [384, 4, 8192], P(('rep', 'fsdp'), None, 'tp')
The draws below stay inside these ranges and needn't reach their ends.
Inputs may be any that keep to these rules, and one draw needn't show every extreme that they name: lengths[r] is the number of valid cached positions of row r, at most 24.
All inputs are finite; a program needn't handle non-finite values.
Results may differ from the reference program's by a relative error of at most 0.0065.
Values may be sent and summed in bfloat16 or wider, within the bound.
A program may use at most 64 MiB of HBM per device.

```python
import math
import jax
import jax.numpy as jnp
from jax import lax

D = 8192
QH = 64
KVH = 8
HD = 128
ROW_DEV = 48
CACHE = 24
STEPS = 4
ROWS = 384
KVW = 1024
N_FSDP = 2


def shared_cache(key):
    base = jax.random.normal(jax.random.fold_in(key, 11), (ROWS, CACHE, 2, KVH * HD), jnp.float32)
    base = jnp.clip(base, -4.0, 4.0)
    return base


def draw_kv_cache(key, part):
    return shared_cache(key).astype(jnp.bfloat16)


def draw_queries(key, part):
    drawn = jax.random.normal(jax.random.fold_in(key, 12), (ROWS, STEPS, QH * HD), jnp.float32)
    drawn = jnp.clip(drawn, -4.0, 4.0)
    return drawn.astype(jnp.bfloat16)


def set_ends(array, key, smallest, top_value):
    extent = array.shape
    index_at = [jax.random.randint(jax.random.fold_in(key, axis), (), 0, extent[axis]) for axis in range(len(extent))]
    array = array.at[tuple(index_at)].set(smallest)
    longest = extent.index(max(extent))
    index_at[longest] = (index_at[longest] + 1) % extent[longest]
    return array.at[tuple(index_at)].set(top_value)


def spiked(drawn, stream_key, source, target, shards_of, factor):
    owner, partner = [(jnp.arange(drawn.shape[position]) // (drawn.shape[position] // shards_of)).reshape([-1 if axis == position else 1 for axis in range(drawn.ndim)]) for position in (source, target)]
    chosen = jax.random.permutation(stream_key, shards_of)[partner]
    strong = (owner == chosen) | (owner == (partner + shards_of // 2) % shards_of)
    return jnp.where(strong, factor * drawn, drawn)


def block_scale(stream_key, dims, split, smallest, largest):
    gain, own = 1.0, jax.random.fold_in(stream_key, 6)
    for position, blocks in split:
        steps = jnp.exp(jax.random.uniform(jax.random.fold_in(own, position), (blocks,), jnp.float32, smallest / len(split), largest / len(split)))
        gain = gain * jnp.repeat(steps, dims[position] // blocks).reshape([-1 if axis == position else 1 for axis in range(len(dims))])
    return gain


def noise(key, shape, spread, bound, cuts=(), held_as=jnp.bfloat16):
    gain = block_scale(key, shape, cuts, -0.22, 0.18) if cuts else 1.0
    array = jax.random.normal(key, shape, jnp.float32) * spread * gain
    return jnp.minimum(jnp.maximum(array, -bound), bound).astype(held_as)


def bell_draw_with(key, dims, spread, most, cuts, heavy, kind=jnp.bfloat16):
    values = spread * jax.random.normal(key, dims, jnp.float32)
    if cuts:
        values = values * block_scale(key, dims, cuts, -0.22, 0.18)
    return jnp.clip(spiked(values, jax.random.fold_in(key, 3), *heavy), -most, most).astype(kind)


def setup_inputs(seed: int = 0) -> dict:
    splits = jax.random.split(jax.random.key(seed), 9)
    grad_parts = bell_draw_with(splits[0], (N_FSDP, 2, D, KVW), 0.5, 4.0, ((0, 2), (2, 4), (3, 4)), (0, 2, 2, 2.0))
    master_weight = noise(splits[1], (2, D, KVW), D ** -0.5, 0.0625, ((1, 8), (2, 4)), jnp.float32)
    moment_one = noise(splits[2], (2, D, KVW), 0.3, 4.0, ((1, 8), (2, 4)), jnp.float32)
    moment_two = jnp.clip(jnp.exp(math.log(2.0) - 2.9957323 * jax.random.uniform(splits[3], (2, D, KVW), jnp.float32) ** block_scale(splits[3], (2, D, KVW), ((1, 8), (2, 4)), -0.2, 0.2)), 0.1, 2.0)
    layer_inputs = noise(splits[4], (ROWS, STEPS, D), 1.0, 6.0, ((0, 8), (2, 4)))
    queries = draw_queries(jax.random.fold_in(splits[8], 71), 0)
    kv_cache = draw_kv_cache(jax.random.fold_in(splits[8], 71), 0)
    lengths = set_ends(jax.random.randint(splits[7], (ROWS,), 2, CACHE + 1), jax.random.fold_in(splits[7], 1), 2, CACHE).astype(jnp.int32)
    return {"grad_parts": grad_parts, "master_weight": master_weight, "moment_one": moment_one, "moment_two": moment_two, "layer_inputs": layer_inputs, "queries": queries, "kv_cache": kv_cache, "lengths": lengths}


beta_one = 0.9
beta_two = 0.95
learning_rate = 0.001
weight_decay = 0.1
epsilon = 1e-08
first_bias = 1.0 - 0.9 ** 10
second_bias = 1.0 - 0.95 ** 10

def adamw_update(gradient, master, moment_one, moment_two):
    new_one = beta_one * moment_one + (1.0 - beta_one) * gradient
    new_two = beta_two * moment_two + (1.0 - beta_two) * gradient * gradient
    update = new_one / first_bias / (jnp.sqrt(new_two / second_bias) + epsilon)
    new_master = master - learning_rate * (update + weight_decay * master)
    return (new_one, new_two, new_master)

def attend(pieces):
    query_block, cache_block, fresh_keys, fresh_values, length_block = pieces
    row_count = query_block.shape[0]
    step_count = query_block.shape[1]
    kv_heads = fresh_keys.shape[2]
    cache_len = cache_block.shape[1]
    grouped = query_block.reshape(row_count, step_count, kv_heads, -1, HD).astype(jnp.float32)
    cached_keys = cache_block[:, :, 0].reshape(row_count, cache_len, kv_heads, HD).astype(jnp.float32)
    cached_values = cache_block[:, :, 1].reshape(row_count, cache_len, kv_heads, HD).astype(jnp.float32)
    scaling = 1.0 / jnp.sqrt(jnp.float32(HD))
    cached_scores = jnp.einsum('rsgqd,rcgd->rsgqc', grouped, cached_keys) * scaling
    fresh_scores = jnp.einsum('rsgqd,rugd->rsgqu', grouped, fresh_keys.astype(jnp.float32)) * scaling
    valid_old = jnp.arange(cache_len, dtype=jnp.int32)[None, :] < length_block[:, None]
    valid_old = valid_old[:, None, None, None, :]
    steps_index = jnp.arange(step_count, dtype=jnp.int32)
    valid_new = (steps_index[None, :] <= steps_index[:, None])[None, :, None, None, :]
    scores = jnp.concatenate([jnp.where(valid_old, cached_scores, -jnp.inf), jnp.where(valid_new, fresh_scores, -jnp.inf)], axis=-1)
    row_max = lax.optimization_barrier(jnp.max(scores, axis=-1, keepdims=True))
    exponent = jnp.exp(scores - row_max)
    weights = (exponent / lax.optimization_barrier(jnp.sum(exponent, axis=-1, keepdims=True))).astype(jnp.bfloat16).astype(jnp.float32)
    output = jnp.einsum('rsgqc,rcgd->rsgqd', weights[..., :cache_len], cached_values)
    output = output + jnp.einsum('rsgqu,rugd->rsgqd', weights[..., cache_len:], fresh_values.astype(jnp.float32))
    return output.astype(jnp.bfloat16).reshape(row_count, step_count, -1)

def reference(grad_parts, master_weight, moment_one, moment_two, layer_inputs, queries, kv_cache, lengths):
    gradient = lax.optimization_barrier(jnp.sum(grad_parts.astype(jnp.float32), axis=0))
    new_one, new_two, new_master = adamw_update(gradient, master_weight, moment_one, moment_two)
    rollout_weight = new_master.astype(jnp.bfloat16)
    flattened = layer_inputs.reshape(ROWS * STEPS, D)
    fresh_keys = jnp.dot(flattened, rollout_weight[0], preferred_element_type=jnp.float32).astype(jnp.bfloat16)
    fresh_values = jnp.dot(flattened, rollout_weight[1], preferred_element_type=jnp.float32).astype(jnp.bfloat16)
    blocks = ROWS // ROW_DEV
    pieces = (queries.reshape(blocks, ROW_DEV, STEPS, QH * HD), kv_cache.reshape(blocks, ROW_DEV, CACHE, 2, KVH * HD), fresh_keys.reshape(blocks, ROW_DEV, STEPS, KVH, HD), fresh_values.reshape(blocks, ROW_DEV, STEPS, KVH, HD), lengths.reshape(blocks, ROW_DEV))
    context = lax.map(attend, pieces).reshape(ROWS, STEPS, QH * HD)
    return (new_master, new_one, new_two, context)
```

```python
import functools

import jax
import jax.numpy as jnp
from jax import lax
from jax.experimental import pallas as pl
from jax.experimental.pallas import tpu as pltpu
from jax.sharding import PartitionSpec as P

MESH = pl.DeviceIdType.MESH
W_CHUNKS = 4
ADAM_SUB = 32
TAIL_STEPS = 4


def learner_kernel(
    sizes, grad_hbm, master_hbm, one_hbm, two_hbm, x_hbm,
    fresh_out, master_out, one_out, two_out,
    own_grad, peer_grad, master, one, two, wbuf, xbuf, acc, partner_acc,
    local_sem, out_sem, grad_send, grad_recv, x_send, x_recv, x_swap_send,
    w_send, w_recv, w_fwd_send, acc_send, acc_recv,
):
    n_tp, depth = sizes
    r, f, t = lax.axis_index("rep"), lax.axis_index("fsdp"), lax.axis_index("tp")
    nf = 1 - f
    rx = r + 1 - 2 * lax.rem(r, 2)
    ry = lax.rem(r + 2, 4)
    rd = lax.rem(rx + 2, 4)
    partner, dev_x, dev_y = (r, nf, t), (rx, f, t), (ry, f, t)
    up, down = (r, f, t + 1), (r, f, t - 1)
    chunk = depth // W_CHUNKS

    def half(index):
        return pl.ds(pl.multiple_of(index * depth, depth), depth)

    local = [
        pltpu.make_async_copy(grad_hbm.at[0, :, half(f), :], own_grad, local_sem.at[0]),
        pltpu.make_async_copy(master_hbm, master, local_sem.at[1]),
        pltpu.make_async_copy(one_hbm, one, local_sem.at[2]),
        pltpu.make_async_copy(two_hbm, two, local_sem.at[3]),
        pltpu.make_async_copy(x_hbm.at[:, half(f)], xbuf.at[t, f], local_sem.at[4]),
    ]
    for copy in local:
        copy.start()

    barrier = pltpu.get_barrier_semaphore()
    for device in (partner, dev_x, dev_y):
        pl.semaphore_signal(barrier, inc=1, device_id=device, device_id_type=MESH)

    @pl.when(t < n_tp - 1)
    def _():
        pl.semaphore_signal(barrier, inc=1, device_id=up, device_id_type=MESH)

    @pl.when(t > 0)
    def _():
        pl.semaphore_signal(barrier, inc=1, device_id=down, device_id_type=MESH)

    pl.semaphore_wait(barrier, jnp.where((t > 0) & (t < n_tp - 1), 5, 4))

    def rows(c):
        return pl.ds(pl.multiple_of(c * chunk, chunk), chunk)

    def remote(src, dst, send, recv, device):
        return pltpu.make_async_remote_copy(
            src_ref=src, dst_ref=dst, send_sem=send, recv_sem=recv,
            device_id=device, device_id_type=MESH,
        )

    def grad_copy(c):
        source = pl.ds(pl.multiple_of(nf * depth + c * chunk, chunk), chunk)
        return remote(
            grad_hbm.at[0, :, source, :], peer_grad.at[:, rows(c), :],
            grad_send.at[c], grad_recv.at[c], partner,
        )

    def x_move(z, th, side):
        return remote(
            xbuf.at[z, th], xbuf.at[z, th], x_send.at[side, z, th], x_recv.at[z, th],
            up if side == 1 else down,
        )

    def x_own(side):
        return remote(
            x_hbm.at[:, half(f)], xbuf.at[t, f], x_send.at[side, t, f], x_recv.at[t, f],
            up if side == 1 else down,
        )

    x_swap = remote(x_hbm.at[:, half(nf)], xbuf.at[t, f], x_swap_send.at[0], x_recv.at[t, f], partner)

    def both_ways(act):
        @pl.when(t < n_tp - 1)
        def _():
            act(1)

        @pl.when(t > 0)
        def _():
            act(0)

    grad_copy(0).start()
    x_swap.start()
    both_ways(lambda side: x_own(side).start())
    for c in range(1, W_CHUNKS):
        grad_copy(c).start()

    def w_copy(c, way):
        return remote(
            wbuf.at[r, :, rows(c), :], wbuf.at[r, :, rows(c), :],
            w_send.at[way, c], w_recv.at[r, c], dev_x if way == 0 else dev_y,
        )

    def w_arrived(owner, c):
        remote(
            wbuf.at[owner, :, rows(c), :], wbuf.at[owner, :, rows(c), :],
            w_send.at[0, c], w_recv.at[owner, c], dev_x,
        ).wait_recv()

    def w_forward(c):
        owner, device = (rx, dev_y) if c % 2 == 0 else (ry, dev_x)
        return remote(
            wbuf.at[owner, :, rows(c), :], wbuf.at[owner, :, rows(c), :],
            w_fwd_send.at[c], w_recv.at[owner, c], device,
        )

    def x_arrived(z, th):
        x_move(z, th, 1).wait_recv()

    for copy in local[:4]:
        copy.wait()

    first_bias = 1.0 - 0.9**10
    second_bias = 1.0 - 0.95**10

    def adam(c):
        def sub(i, carry):
            at = pl.ds(pl.multiple_of(c * chunk + i * ADAM_SUB, ADAM_SUB), ADAM_SUB)
            gradient = own_grad[:, at, :].astype(jnp.float32) + peer_grad[:, at, :].astype(jnp.float32)
            new_one = 0.9 * one[:, at, :] + (1.0 - 0.9) * gradient
            new_two = 0.95 * two[:, at, :] + (1.0 - 0.95) * gradient * gradient
            update = new_one / first_bias / (jnp.sqrt(new_two / second_bias) + 1e-08)
            old = master[:, at, :]
            new_master = old - 0.001 * (update + 0.1 * old)
            one[:, at, :] = new_one
            two[:, at, :] = new_two
            master[:, at, :] = new_master
            wbuf[r, :, at, :] = new_master.astype(jnp.bfloat16)
            return carry

        lax.fori_loop(0, chunk // ADAM_SUB, sub, 0)

    for c in range(W_CHUNKS):
        grad_copy(c).wait_recv()
        adam(c)
        if c == 0:
            x_arrived(t, nf)
            both_ways(lambda side: x_move(t, nf, side).start())
        else:
            w_copy(c - 1, 0).start()
            w_copy(c - 1, 1).start()
    outs = [
        pltpu.make_async_copy(master, master_out, out_sem.at[0]),
        pltpu.make_async_copy(one, one_out, out_sem.at[1]),
        pltpu.make_async_copy(two, two_out, out_sem.at[2]),
    ]
    for copy in outs:
        copy.start()
    w_copy(W_CHUNKS - 1, 0).start()
    w_copy(W_CHUNKS - 1, 1).start()
    local[4].wait()

    def x_step(k, th):
        @pl.when(t - k >= 0)
        def _():
            x_arrived(t - k, th)

            @pl.when(t < n_tp - 1)
            def _():
                x_move(t - k, th, 1).start()

        @pl.when(t + k < n_tp)
        def _():
            x_arrived(t + k, th)

            @pl.when(t > 0)
            def _():
                x_move(t + k, th, 0).start()

    def w_step(c):
        w_arrived(rx, c)
        w_arrived(ry, c)
        w_forward(c).start()

    x_step(1, f)
    w_step(0)
    x_step(1, nf)
    w_step(1)
    w_step(2)
    x_step(2, f)
    w_step(3)
    x_step(2, nf)

    acc[...] = jnp.zeros_like(acc)

    def multiply(z, th):
        def one_side(kv, carry):
            acc[th, kv] += jnp.dot(xbuf[z, th], wbuf[z, kv], preferred_element_type=jnp.float32)
            return carry

        lax.fori_loop(0, 2, one_side, 0)

    for c in range(W_CHUNKS):
        w_arrived(rd, c)

    def step(j, carry):
        k = j // 2
        th = f + lax.rem(j, 2) * (1 - 2 * f)

        def side(s, inner):
            z = t + (2 * s - 1) * k

            @pl.when((z >= 0) & (z < n_tp))
            def _():
                @pl.when(k == n_tp - 1)
                def _():
                    x_arrived(z, th)

                multiply(z, th)

            return inner

        lax.fori_loop(jnp.where(k == 0, 1, 0), 2, side, 0)
        return carry

    lax.fori_loop(0, 2 * n_tp, step, 0)

    swap = remote(acc.at[nf], partner_acc, acc_send.at[0], acc_recv.at[0], partner)
    swap.start()
    for c in range(W_CHUNKS):
        grad_copy(c).wait_send()
        w_copy(c, 0).wait_send()
        w_copy(c, 1).wait_send()
        w_forward(c).wait_send()
    x_swap.wait_send()
    both_ways(lambda side: x_own(side).wait_send())
    both_ways(lambda side: x_move(t, nf, side).wait_send())
    for k in range(1, n_tp - 1):
        for th in (f, nf):
            @pl.when((t - k >= 0) & (t < n_tp - 1))
            def _():
                x_move(t - k, th, 1).wait_send()

            @pl.when((t + k < n_tp) & (t > 0))
            def _():
                x_move(t + k, th, 0).wait_send()
    for copy in outs:
        copy.wait()
    swap.wait_recv()
    fresh_out[...] = (acc[f] + partner_acc[...]).astype(jnp.bfloat16)
    swap.wait_send()


def tail_kernel(
    shape, lengths, q_ref, kv_ref, fresh_ref, master_in, one_in, two_in,
    context, master_out, one_out, two_out,
):
    row_count, step_count, cache_len, head = shape
    block = pl.program_id(0)
    master_out[...] = master_in[...]
    one_out[...] = one_in[...]
    two_out[...] = two_in[...]
    tokens = row_count * step_count
    cached = row_count * cache_len
    groups = fresh_ref.shape[2] // head
    per_group = q_ref.shape[1] // head // groups
    key_row = lax.broadcasted_iota(jnp.int32, (1, cached), 1) // cache_len
    position = lax.broadcasted_iota(jnp.int32, (1, cached), 1) - key_row * cache_len
    limit = jnp.zeros((1, cached), jnp.int32)
    for row in range(row_count):
        limit = jnp.where(key_row == row, lengths[block * row_count + row], limit)
    key_row = jnp.where(position < limit, key_row, -1)
    token = lax.broadcasted_iota(jnp.int32, (tokens, 1), 0)
    old_ok = key_row == token // step_count
    fresh = lax.broadcasted_iota(jnp.int32, (1, tokens), 1)
    new_ok = (fresh // step_count == token // step_count) & (fresh <= token)
    scale = head**-0.5
    low = -0.7 * float(jnp.finfo(jnp.float32).max)
    contract = (((1,), (1,)), ((), ()))
    for group in range(groups):
        cols = slice(group * head, (group + 1) * head)
        vcols = slice((groups + group) * head, (groups + group + 1) * head)
        query = jnp.concatenate(
            [
                q_ref[:, (group * per_group + h) * head : (group * per_group + h + 1) * head]
                for h in range(per_group)
            ],
            axis=0,
        )
        old = lax.dot_general(query, kv_ref[:, cols], contract, preferred_element_type=jnp.float32)
        new = lax.dot_general(query, fresh_ref[0, :, cols], contract, preferred_element_type=jnp.float32)
        old = jnp.where(old_ok[None], old.reshape(per_group, tokens, cached) * scale, low)
        new = jnp.where(new_ok[None], new.reshape(per_group, tokens, tokens) * scale, low)
        top = jnp.maximum(jnp.max(old, axis=-1, keepdims=True), jnp.max(new, axis=-1, keepdims=True))
        old = jnp.exp(old - top)
        new = jnp.exp(new - top)
        total = jnp.sum(old, axis=-1, keepdims=True) + jnp.sum(new, axis=-1, keepdims=True)
        old = (old / total).astype(jnp.bfloat16).reshape(per_group * tokens, cached)
        new = (new / total).astype(jnp.bfloat16).reshape(per_group * tokens, tokens)
        out = jnp.dot(old, kv_ref[:, vcols], preferred_element_type=jnp.float32)
        out = out + jnp.dot(new, fresh_ref[1, :, cols], preferred_element_type=jnp.float32)
        out = out.astype(jnp.bfloat16)
        for h in range(per_group):
            at = (group * per_group + h) * head
            context[:, at : at + head] = out[h * tokens : (h + 1) * tokens]


def fused_device(head, n_rep, grad_parts, master_weight, moment_one, moment_two, layer_inputs, queries, kv_cache, lengths):
    row_count, step_count, features = layer_inputs.shape
    _, depth, width = master_weight.shape
    n_tp = n_rep
    tokens = row_count * step_count
    cache_len = kv_cache.shape[1]
    bf16, f32 = jnp.bfloat16, jnp.float32
    dma = pltpu.SemaphoreType.DMA
    state = jax.ShapeDtypeStruct(master_weight.shape, f32)
    any_spec = pl.BlockSpec(memory_space=pl.ANY)
    fresh, master, one, two = pl.pallas_call(
        functools.partial(learner_kernel, (n_tp, depth)),
        out_shape=(jax.ShapeDtypeStruct((2, tokens, width), bf16), state, state, state),
        in_specs=[any_spec] * 5,
        out_specs=(pl.BlockSpec(memory_space=pltpu.VMEM), any_spec, any_spec, any_spec),
        scratch_shapes=[
            pltpu.VMEM((2, depth, width), bf16),
            pltpu.VMEM((2, depth, width), bf16),
            pltpu.VMEM((2, depth, width), f32),
            pltpu.VMEM((2, depth, width), f32),
            pltpu.VMEM((2, depth, width), f32),
            pltpu.VMEM((n_rep, 2, depth, width), bf16),
            pltpu.VMEM((n_tp, 2, tokens, depth), bf16),
            pltpu.VMEM((2, 2, tokens, width), f32),
            pltpu.VMEM((2, tokens, width), f32),
            dma((5,)),
            dma((3,)),
            dma((W_CHUNKS,)),
            dma((W_CHUNKS,)),
            dma((2, n_tp, 2)),
            dma((n_tp, 2)),
            dma((1,)),
            dma((2, W_CHUNKS)),
            dma((n_rep, W_CHUNKS)),
            dma((W_CHUNKS,)),
            dma((1,)),
            dma((1,)),
        ],
        compiler_params=pltpu.CompilerParams(
            collective_id=0, has_side_effects=True, vmem_limit_bytes=40 * 1024 * 1024
        ),
    )(grad_parts, master_weight, moment_one, moment_two, layer_inputs.reshape(tokens, features))
    block_rows = row_count // TAIL_STEPS
    block_tokens = tokens // TAIL_STEPS
    state_spec = pl.BlockSpec((2, depth // TAIL_STEPS, width), lambda i, *_: (0, i, 0))
    token_spec = pl.BlockSpec((block_tokens, features), lambda i, *_: (i, 0))
    context, master, one, two = pl.pallas_call(
        functools.partial(tail_kernel, (block_rows, step_count, cache_len, head)),
        out_shape=(jax.ShapeDtypeStruct((tokens, features), bf16), state, state, state),
        grid_spec=pltpu.PrefetchScalarGridSpec(
            num_scalar_prefetch=1,
            grid=(TAIL_STEPS,),
            in_specs=[
                token_spec,
                pl.BlockSpec((block_rows * cache_len, 2 * width), lambda i, *_: (i, 0)),
                pl.BlockSpec((2, block_tokens, width), lambda i, *_: (0, i, 0)),
                state_spec,
                state_spec,
                state_spec,
            ],
            out_specs=(token_spec, state_spec, state_spec, state_spec),
        ),
        compiler_params=pltpu.CompilerParams(dimension_semantics=("arbitrary",)),
    )(
        lengths,
        queries.reshape(tokens, features),
        kv_cache.reshape(row_count * cache_len, 2 * width),
        fresh,
        master,
        one,
        two,
    )
    return (master, one, two, context.reshape(queries.shape))


HD = 128


beta_one = 0.9
beta_two = 0.95
learning_rate = 0.001
weight_decay = 0.1
epsilon = 1e-08
first_bias = 1.0 - 0.9**10
second_bias = 1.0 - 0.95**10


def adamw_update(gradient, master, moment_one, moment_two):
    new_one = beta_one * moment_one + (1.0 - beta_one) * gradient
    new_two = beta_two * moment_two + (1.0 - beta_two) * gradient * gradient
    update = new_one / first_bias / (jnp.sqrt(new_two / second_bias) + epsilon)
    new_master = master - learning_rate * (update + weight_decay * master)
    return (new_one, new_two, new_master)


def attend(queries, kv_cache, fresh_keys, fresh_values, lengths):
    row_count = queries.shape[0]
    step_count = queries.shape[1]
    kv_heads = fresh_keys.shape[2]
    cache_len = kv_cache.shape[1]
    grouped = queries.reshape(row_count, step_count, kv_heads, -1, HD)
    cached_keys = kv_cache[:, :, 0].reshape(row_count, cache_len, kv_heads, HD)
    cached_values = kv_cache[:, :, 1].reshape(row_count, cache_len, kv_heads, HD)
    scaling = 1.0 / jnp.sqrt(jnp.float32(HD))
    cached_scores = (
        jnp.einsum("rsgqd,rcgd->rsgqc", grouped, cached_keys, preferred_element_type=jnp.float32)
        * scaling
    )
    fresh_scores = (
        jnp.einsum("rsgqd,rugd->rsgqu", grouped, fresh_keys, preferred_element_type=jnp.float32)
        * scaling
    )
    valid_old = jnp.arange(cache_len, dtype=jnp.int32)[None, :] < lengths[:, None]
    valid_old = valid_old[:, None, None, None, :]
    steps_index = jnp.arange(step_count, dtype=jnp.int32)
    valid_new = (steps_index[None, :] <= steps_index[:, None])[None, :, None, None, :]
    scores = jnp.concatenate(
        [
            jnp.where(valid_old, cached_scores, -jnp.inf),
            jnp.where(valid_new, fresh_scores, -jnp.inf),
        ],
        axis=-1,
    )
    row_max = jnp.max(scores, axis=-1, keepdims=True)
    exponent = jnp.exp(scores - row_max)
    weights = (exponent / jnp.sum(exponent, axis=-1, keepdims=True)).astype(jnp.bfloat16)
    output = jnp.einsum(
        "rsgqc,rcgd->rsgqd",
        weights[..., :cache_len],
        cached_values,
        preferred_element_type=jnp.float32,
    )
    output = output + jnp.einsum(
        "rsgqu,rugd->rsgqd",
        weights[..., cache_len:],
        fresh_values,
        preferred_element_type=jnp.float32,
    )
    return output.astype(jnp.bfloat16).reshape(row_count, step_count, -1)


def on_device(
    grad_parts, master_weight, moment_one, moment_two, layer_inputs, queries, kv_cache, lengths
):
    gradient = lax.psum_scatter(
        grad_parts[0].astype(jnp.float32).astype(jnp.bfloat16),
        "fsdp",
        scatter_dimension=1,
        tiled=True,
    ).astype(jnp.float32)
    new_one, new_two, new_master = adamw_update(gradient, master_weight, moment_one, moment_two)
    rollout_weight = new_master.astype(jnp.bfloat16)
    row_count = layer_inputs.shape[0]
    step_count = layer_inputs.shape[1]
    gathered = lax.all_gather(layer_inputs, "tp", axis=2, tiled=True)
    flattened = gathered.reshape(row_count * step_count, gathered.shape[2])
    projected = jnp.einsum(
        "td,kdc->ktc",
        flattened,
        lax.all_gather(rollout_weight, ("rep", "fsdp"), axis=1, tiled=True),
        preferred_element_type=jnp.float32,
    )
    fresh_pair = projected.astype(jnp.bfloat16).reshape(2, row_count, step_count, -1, HD)
    context = attend(queries, kv_cache, fresh_pair[0], fresh_pair[1], lengths)
    return (new_master, new_one, new_two, context)


def solution(mesh):
    shape = mesh.shape
    fits = shape["rep"] == 4 and shape["tp"] == 4 and shape["fsdp"] == 2
    run = functools.partial(fused_device, HD, shape["rep"]) if fits else on_device
    return jax.shard_map(
        run,
        mesh=mesh,
        in_specs=(
            P("fsdp", None, "rep", "tp"),
            P(None, ("rep", "fsdp"), "tp"),
            P(None, ("rep", "fsdp"), "tp"),
            P(None, ("rep", "fsdp"), "tp"),
            P(("rep", "fsdp"), None, "tp"),
            P(("rep", "fsdp"), None, "tp"),
            P(("rep", "fsdp"), None, None, "tp"),
            P(("rep", "fsdp")),
        ),
        out_specs=(
            P(None, ("rep", "fsdp"), "tp"),
            P(None, ("rep", "fsdp"), "tp"),
            P(None, ("rep", "fsdp"), "tp"),
            P(("rep", "fsdp"), None, "tp"),
        ),
        check_vma=False,
    )
```

```python
import functools

import jax
import jax.numpy as jnp
from jax import lax
from jax.experimental import pallas as pl
from jax.experimental.pallas import tpu as pltpu
from jax.sharding import PartitionSpec as P

HD = 128
MESH = pl.DeviceIdType.MESH
W_CHUNKS = 4
ADAM_SUB = 32
TAIL_ROWS = 8


def learner_kernel(
    sizes, grad_hbm, master_hbm, one_hbm, two_hbm, x_hbm, kv_hbm,
    fresh_out, cached_out, master_out, one_out, two_out,
    own_grad, peer_grad, master, one, two, wbuf, xbuf, xflat, acc, partner_acc, kv_raw, kv_flat,
    local_sem, out_sem, grad_send, grad_recv, x_send, x_recv, x_swap_send,
    w_send, w_recv, w_fwd_send, acc_send, acc_recv,
):
    n_tp, depth = sizes
    r, f, t = lax.axis_index("rep"), lax.axis_index("fsdp"), lax.axis_index("tp")
    nf = 1 - f
    rx = r + 1 - 2 * lax.rem(r, 2)
    ry = lax.rem(r + 2, 4)
    rd = lax.rem(rx + 2, 4)
    partner, dev_x, dev_y = (r, nf, t), (rx, f, t), (ry, f, t)
    up, down = (r, f, t + 1), (r, f, t - 1)
    chunk = depth // W_CHUNKS

    def half(index):
        return pl.ds(pl.multiple_of(index * depth, depth), depth)

    local = [
        pltpu.make_async_copy(grad_hbm.at[0, :, half(f), :], own_grad, local_sem.at[0]),
        pltpu.make_async_copy(master_hbm, master, local_sem.at[1]),
        pltpu.make_async_copy(one_hbm, one, local_sem.at[2]),
        pltpu.make_async_copy(two_hbm, two, local_sem.at[3]),
        pltpu.make_async_copy(x_hbm.at[:, :, half(f)], xbuf.at[t, f], local_sem.at[4]),
        pltpu.make_async_copy(kv_hbm, kv_raw, local_sem.at[5]),
    ]
    for copy in local:
        copy.start()

    barrier = pltpu.get_barrier_semaphore()
    for device in (partner, dev_x, dev_y):
        pl.semaphore_signal(barrier, inc=1, device_id=device, device_id_type=MESH)

    @pl.when(t < n_tp - 1)
    def _():
        pl.semaphore_signal(barrier, inc=1, device_id=up, device_id_type=MESH)

    @pl.when(t > 0)
    def _():
        pl.semaphore_signal(barrier, inc=1, device_id=down, device_id_type=MESH)

    pl.semaphore_wait(barrier, jnp.where((t > 0) & (t < n_tp - 1), 5, 4))

    def rows(c):
        return pl.ds(pl.multiple_of(c * chunk, chunk), chunk)

    def remote(src, dst, send, recv, device):
        return pltpu.make_async_remote_copy(
            src_ref=src, dst_ref=dst, send_sem=send, recv_sem=recv,
            device_id=device, device_id_type=MESH,
        )

    def grad_copy(c):
        source = pl.ds(pl.multiple_of(nf * depth + c * chunk, chunk), chunk)
        return remote(
            grad_hbm.at[0, :, source, :], peer_grad.at[:, rows(c), :],
            grad_send.at[c], grad_recv.at[c], partner,
        )

    def x_move(z, th, side):
        return remote(
            xbuf.at[z, th], xbuf.at[z, th], x_send.at[side, z, th], x_recv.at[z, th],
            up if side == 1 else down,
        )

    def x_own(side):
        return remote(
            x_hbm.at[:, :, half(f)], xbuf.at[t, f], x_send.at[side, t, f], x_recv.at[t, f],
            up if side == 1 else down,
        )

    x_swap = remote(x_hbm.at[:, :, half(nf)], xbuf.at[t, f], x_swap_send.at[0], x_recv.at[t, f], partner)

    def both_ways(act):
        @pl.when(t < n_tp - 1)
        def _():
            act(1)

        @pl.when(t > 0)
        def _():
            act(0)

    grad_copy(0).start()
    x_swap.start()
    both_ways(lambda side: x_own(side).start())
    for c in range(1, W_CHUNKS):
        grad_copy(c).start()

    def w_copy(c, way):
        return remote(
            wbuf.at[r, :, rows(c), :], wbuf.at[r, :, rows(c), :],
            w_send.at[way, c], w_recv.at[r, c], dev_x if way == 0 else dev_y,
        )

    def w_arrived(owner, c):
        remote(
            wbuf.at[owner, :, rows(c), :], wbuf.at[owner, :, rows(c), :],
            w_send.at[0, c], w_recv.at[owner, c], dev_x,
        ).wait_recv()

    def w_forward(c):
        owner, device = (rx, dev_y) if c % 2 == 0 else (ry, dev_x)
        return remote(
            wbuf.at[owner, :, rows(c), :], wbuf.at[owner, :, rows(c), :],
            w_fwd_send.at[c], w_recv.at[owner, c], device,
        )

    def x_arrived(z, th):
        x_move(z, th, 1).wait_recv()

    for copy in local[:4]:
        copy.wait()

    first_bias = 1.0 - 0.9**10
    second_bias = 1.0 - 0.95**10

    def adam(c):
        def sub(i, carry):
            at = pl.ds(pl.multiple_of(c * chunk + i * ADAM_SUB, ADAM_SUB), ADAM_SUB)
            gradient = own_grad[:, at, :].astype(jnp.float32) + peer_grad[:, at, :].astype(jnp.float32)
            new_one = 0.9 * one[:, at, :] + (1.0 - 0.9) * gradient
            new_two = 0.95 * two[:, at, :] + (1.0 - 0.95) * gradient * gradient
            update = new_one / first_bias / (jnp.sqrt(new_two / second_bias) + 1e-08)
            old = master[:, at, :]
            new_master = old - 0.001 * (update + 0.1 * old)
            one[:, at, :] = new_one
            two[:, at, :] = new_two
            master[:, at, :] = new_master
            wbuf[r, :, at, :] = new_master.astype(jnp.bfloat16)
            return carry

        lax.fori_loop(0, chunk // ADAM_SUB, sub, 0)

    for c in range(W_CHUNKS):
        grad_copy(c).wait_recv()
        adam(c)
        if c == 0:
            x_arrived(t, nf)
            both_ways(lambda side: x_move(t, nf, side).start())
        else:
            w_copy(c - 1, 0).start()
            w_copy(c - 1, 1).start()
    outs = [
        pltpu.make_async_copy(master, master_out, out_sem.at[0]),
        pltpu.make_async_copy(one, one_out, out_sem.at[1]),
        pltpu.make_async_copy(two, two_out, out_sem.at[2]),
    ]
    for copy in outs:
        copy.start()
    w_copy(W_CHUNKS - 1, 0).start()
    w_copy(W_CHUNKS - 1, 1).start()
    local[4].wait()
    local[5].wait()

    def x_step(k, th):
        @pl.when(t - k >= 0)
        def _():
            x_arrived(t - k, th)

            @pl.when(t < n_tp - 1)
            def _():
                x_move(t - k, th, 1).start()

        @pl.when(t + k < n_tp)
        def _():
            x_arrived(t + k, th)

            @pl.when(t > 0)
            def _():
                x_move(t + k, th, 0).start()

    def w_step(c):
        w_arrived(rx, c)
        w_arrived(ry, c)
        w_forward(c).start()

    kv_rows, cache_len = kv_raw.shape[:2]
    pieces = kv_rows // 8

    def split_cache(quarter):
        def body(i, carry):
            row = (quarter * pieces + i) * 2
            at = pl.ds(pl.multiple_of(row * cache_len, 2 * cache_len), 2 * cache_len)
            for j in range(2):
                kv_flat[j, at, :] = kv_raw[pl.ds(row, 2), :, j, :].reshape(2 * cache_len, -1)
            return carry

        lax.fori_loop(0, pieces, body, 0)

    split_cache(0)
    x_step(1, f)
    split_cache(1)
    w_step(0)
    split_cache(2)
    x_step(1, nf)
    split_cache(3)
    cached_copy = pltpu.make_async_copy(kv_flat, cached_out, out_sem.at[3])
    cached_copy.start()
    w_step(1)
    w_step(2)
    x_step(2, f)
    w_step(3)
    x_step(2, nf)

    acc[...] = jnp.zeros_like(acc)

    x_rows = xbuf.shape[2]
    x_part = x_rows // 4
    flat_part = xflat.shape[0] // 4

    def multiply(z, th):
        def flatten(i, carry):
            at = pl.ds(pl.multiple_of(i * flat_part, flat_part), flat_part)
            xflat[at, :] = xbuf[z, th, pl.ds(i * x_part, x_part)].reshape(flat_part, depth)
            return carry

        lax.fori_loop(0, 4, flatten, 0)

        def one_side(kv, carry):
            acc[th, kv] += jnp.dot(xflat[...], wbuf[z, kv], preferred_element_type=jnp.float32)
            return carry

        lax.fori_loop(0, 2, one_side, 0)

    for c in range(W_CHUNKS):
        w_arrived(rd, c)

    def step(j, carry):
        k = j // 2
        th = f + lax.rem(j, 2) * (1 - 2 * f)

        def side(s, inner):
            z = t + (2 * s - 1) * k

            @pl.when((z >= 0) & (z < n_tp))
            def _():
                @pl.when(k == n_tp - 1)
                def _():
                    x_arrived(z, th)

                multiply(z, th)

            return inner

        lax.fori_loop(jnp.where(k == 0, 1, 0), 2, side, 0)
        return carry

    lax.fori_loop(0, 2 * n_tp, step, 0)

    swap = remote(acc.at[nf], partner_acc, acc_send.at[0], acc_recv.at[0], partner)
    swap.start()
    for c in range(W_CHUNKS):
        grad_copy(c).wait_send()
        w_copy(c, 0).wait_send()
        w_copy(c, 1).wait_send()
        w_forward(c).wait_send()
    x_swap.wait_send()
    both_ways(lambda side: x_own(side).wait_send())
    both_ways(lambda side: x_move(t, nf, side).wait_send())
    for k in range(1, n_tp - 1):
        for th in (f, nf):
            @pl.when((t - k >= 0) & (t < n_tp - 1))
            def _():
                x_move(t - k, th, 1).wait_send()

            @pl.when((t + k < n_tp) & (t > 0))
            def _():
                x_move(t + k, th, 0).wait_send()
    for copy in outs:
        copy.wait()
    cached_copy.wait()
    swap.wait_recv()
    fresh_out[...] = (acc[f] + partner_acc[...]).astype(jnp.bfloat16)
    swap.wait_send()


def tail_kernel(
    lengths, q_ref, kv_ref, fresh_in, master_in, one_in, two_in,
    context, master_out, one_out, two_out, fresh_ref, sem,
):
    block = pl.program_id(0)
    moves = [
        pltpu.make_async_copy(master_in, master_out, sem.at[1]),
        pltpu.make_async_copy(one_in, one_out, sem.at[2]),
        pltpu.make_async_copy(two_in, two_out, sem.at[3]),
    ]

    @pl.when(block == 0)
    def _():
        fresh_copy = pltpu.make_async_copy(fresh_in, fresh_ref, sem.at[0])
        fresh_copy.start()
        for move in moves:
            move.start()
        fresh_copy.wait()

    row_count, step_count, features = q_ref.shape
    cached = kv_ref.shape[1]
    head = HD
    cache_len = cached // row_count
    tokens = row_count * step_count
    keys = cached + tokens
    groups = fresh_ref.shape[2] // head
    per_group = features // head // groups
    here = pl.ds(pl.multiple_of(block * tokens, tokens), tokens)
    column = lax.broadcasted_iota(jnp.int32, (1, keys), 1)
    is_old = column < cached
    new_column = column - cached
    key_row = jnp.where(is_old, column // cache_len, new_column // step_count)
    position = column - key_row * cache_len
    limit = jnp.zeros((1, keys), jnp.int32)
    for row in range(row_count):
        limit = jnp.where(key_row == row, lengths[block * row_count + row], limit)
    old_row = jnp.where(is_old & (position < limit), key_row, -1)
    new_row = jnp.where(is_old, -1, key_row)
    token = lax.broadcasted_iota(jnp.int32, (tokens, 1), 0)
    row = token // step_count
    valid = (old_row == row) | ((new_row == row) & (new_column <= token))
    low = -0.7 * float(jnp.finfo(jnp.float32).max)
    contract = (((1,), (1,)), ((), ()))
    for group in range(groups):
        cols = slice(group * head, (group + 1) * head)
        query = jnp.concatenate(
            [
                q_ref[:, :, (group * per_group + h) * head : (group * per_group + h + 1) * head].reshape(tokens, head)
                for h in range(per_group)
            ],
            axis=0,
        )
        key = jnp.concatenate([kv_ref[0, :, cols], fresh_ref[0, here, cols]], axis=0)
        value = jnp.concatenate([kv_ref[1, :, cols], fresh_ref[1, here, cols]], axis=0)
        scores = lax.dot_general(query, key, contract, preferred_element_type=jnp.float32)
        scores = jnp.where(valid[None], scores.reshape(per_group, tokens, keys) * head**-0.5, low)
        weights = jnp.exp(scores - jnp.max(scores, axis=-1, keepdims=True))
        weights = weights * (1.0 / jnp.sum(weights, axis=-1, keepdims=True))
        weights = weights.astype(jnp.bfloat16).reshape(per_group * tokens, keys)
        out = jnp.dot(weights, value, preferred_element_type=jnp.float32)
        for h in range(per_group):
            at = (group * per_group + h) * head
            piece = out[h * tokens : (h + 1) * tokens].reshape(row_count, step_count, head)
            context[:, :, at : at + head] = piece.astype(jnp.bfloat16)

    @pl.when(block == pl.num_programs(0) - 1)
    def _():
        for move in moves:
            move.wait()


def fused_device(n_rep, grad_parts, master_weight, moment_one, moment_two, layer_inputs, queries, kv_cache, lengths):
    row_count, step_count, features = layer_inputs.shape
    _, depth, width = master_weight.shape
    n_tp = n_rep
    tokens = row_count * step_count
    cache_len = kv_cache.shape[1]
    bf16, f32 = jnp.bfloat16, jnp.float32
    dma = pltpu.SemaphoreType.DMA
    state = jax.ShapeDtypeStruct(master_weight.shape, f32)
    any_spec = pl.BlockSpec(memory_space=pl.ANY)
    hbm_spec = pl.BlockSpec(memory_space=pltpu.HBM)
    fresh, cached, master, one, two = pl.pallas_call(
        functools.partial(learner_kernel, (n_tp, depth)),
        out_shape=(
            jax.ShapeDtypeStruct((2, tokens, width), bf16),
            jax.ShapeDtypeStruct((2, row_count * cache_len, width), bf16),
            state,
            state,
            state,
        ),
        in_specs=[hbm_spec] * 6,
        out_specs=(pl.BlockSpec(memory_space=pltpu.VMEM), hbm_spec, any_spec, any_spec, any_spec),
        scratch_shapes=[
            pltpu.VMEM((2, depth, width), bf16),
            pltpu.VMEM((2, depth, width), bf16),
            pltpu.VMEM((2, depth, width), f32),
            pltpu.VMEM((2, depth, width), f32),
            pltpu.VMEM((2, depth, width), f32),
            pltpu.VMEM((n_rep, 2, depth, width), bf16),
            pltpu.VMEM((n_tp, 2, row_count, step_count, depth), bf16),
            pltpu.VMEM((tokens, depth), bf16),
            pltpu.VMEM((2, 2, tokens, width), f32),
            pltpu.VMEM((2, tokens, width), f32),
            pltpu.VMEM(kv_cache.shape, bf16),
            pltpu.VMEM((2, row_count * cache_len, width), bf16),
            dma((6,)),
            dma((4,)),
            dma((W_CHUNKS,)),
            dma((W_CHUNKS,)),
            dma((2, n_tp, 2)),
            dma((n_tp, 2)),
            dma((1,)),
            dma((2, W_CHUNKS)),
            dma((n_rep, W_CHUNKS)),
            dma((W_CHUNKS,)),
            dma((1,)),
            dma((1,)),
        ],
        compiler_params=pltpu.CompilerParams(
            collective_id=0, has_side_effects=True, vmem_limit_bytes=36 * 1024 * 1024
        ),
    )(grad_parts, master_weight, moment_one, moment_two, layer_inputs, kv_cache)
    token_spec = pl.BlockSpec((TAIL_ROWS, step_count, features), lambda i, *_: (i, 0, 0))
    context, master, one, two = pl.pallas_call(
        tail_kernel,
        out_shape=(jax.ShapeDtypeStruct(queries.shape, bf16), state, state, state),
        grid_spec=pltpu.PrefetchScalarGridSpec(
            num_scalar_prefetch=1,
            grid=(row_count // TAIL_ROWS,),
            in_specs=[
                token_spec,
                pl.BlockSpec((2, TAIL_ROWS * cache_len, width), lambda i, *_: (0, i, 0)),
                any_spec,
                any_spec,
                any_spec,
                any_spec,
            ],
            out_specs=(token_spec, hbm_spec, hbm_spec, hbm_spec),
            scratch_shapes=[pltpu.VMEM((2, tokens, width), bf16), dma((4,))],
        ),
        compiler_params=pltpu.CompilerParams(
            dimension_semantics=("arbitrary",), vmem_limit_bytes=16 * 1024 * 1024
        ),
    )(lengths, queries, cached, fresh, master, one, two)
    return (master, one, two, context)


beta_one = 0.9
beta_two = 0.95
learning_rate = 0.001
weight_decay = 0.1
epsilon = 1e-08
first_bias = 1.0 - 0.9**10
second_bias = 1.0 - 0.95**10


def adamw_update(gradient, master, moment_one, moment_two):
    new_one = beta_one * moment_one + (1.0 - beta_one) * gradient
    new_two = beta_two * moment_two + (1.0 - beta_two) * gradient * gradient
    update = new_one / first_bias / (jnp.sqrt(new_two / second_bias) + epsilon)
    new_master = master - learning_rate * (update + weight_decay * master)
    return (new_one, new_two, new_master)


def attend(queries, kv_cache, fresh_keys, fresh_values, lengths):
    row_count = queries.shape[0]
    step_count = queries.shape[1]
    kv_heads = fresh_keys.shape[2]
    cache_len = kv_cache.shape[1]
    grouped = queries.reshape(row_count, step_count, kv_heads, -1, HD)
    cached_keys = kv_cache[:, :, 0].reshape(row_count, cache_len, kv_heads, HD)
    cached_values = kv_cache[:, :, 1].reshape(row_count, cache_len, kv_heads, HD)
    scaling = 1.0 / jnp.sqrt(jnp.float32(HD))
    cached_scores = (
        jnp.einsum("rsgqd,rcgd->rsgqc", grouped, cached_keys, preferred_element_type=jnp.float32)
        * scaling
    )
    fresh_scores = (
        jnp.einsum("rsgqd,rugd->rsgqu", grouped, fresh_keys, preferred_element_type=jnp.float32)
        * scaling
    )
    valid_old = jnp.arange(cache_len, dtype=jnp.int32)[None, :] < lengths[:, None]
    valid_old = valid_old[:, None, None, None, :]
    steps_index = jnp.arange(step_count, dtype=jnp.int32)
    valid_new = (steps_index[None, :] <= steps_index[:, None])[None, :, None, None, :]
    scores = jnp.concatenate(
        [
            jnp.where(valid_old, cached_scores, -jnp.inf),
            jnp.where(valid_new, fresh_scores, -jnp.inf),
        ],
        axis=-1,
    )
    row_max = jnp.max(scores, axis=-1, keepdims=True)
    exponent = jnp.exp(scores - row_max)
    weights = (exponent / jnp.sum(exponent, axis=-1, keepdims=True)).astype(jnp.bfloat16)
    output = jnp.einsum(
        "rsgqc,rcgd->rsgqd",
        weights[..., :cache_len],
        cached_values,
        preferred_element_type=jnp.float32,
    )
    output = output + jnp.einsum(
        "rsgqu,rugd->rsgqd",
        weights[..., cache_len:],
        fresh_values,
        preferred_element_type=jnp.float32,
    )
    return output.astype(jnp.bfloat16).reshape(row_count, step_count, -1)


def on_device(
    grad_parts, master_weight, moment_one, moment_two, layer_inputs, queries, kv_cache, lengths
):
    gradient = lax.psum_scatter(
        grad_parts[0].astype(jnp.float32).astype(jnp.bfloat16),
        "fsdp",
        scatter_dimension=1,
        tiled=True,
    ).astype(jnp.float32)
    new_one, new_two, new_master = adamw_update(gradient, master_weight, moment_one, moment_two)
    rollout_weight = new_master.astype(jnp.bfloat16)
    row_count = layer_inputs.shape[0]
    step_count = layer_inputs.shape[1]
    gathered = lax.all_gather(layer_inputs, "tp", axis=2, tiled=True)
    flattened = gathered.reshape(row_count * step_count, gathered.shape[2])
    projected = jnp.einsum(
        "td,kdc->ktc",
        flattened,
        lax.all_gather(rollout_weight, ("rep", "fsdp"), axis=1, tiled=True),
        preferred_element_type=jnp.float32,
    )
    fresh_pair = projected.astype(jnp.bfloat16).reshape(2, row_count, step_count, -1, HD)
    context = attend(queries, kv_cache, fresh_pair[0], fresh_pair[1], lengths)
    return (new_master, new_one, new_two, context)


def solution(mesh):
    shape = mesh.shape
    fits = shape["rep"] == 4 and shape["tp"] == 4 and shape["fsdp"] == 2
    run = functools.partial(fused_device, shape["rep"]) if fits else on_device
    return jax.shard_map(
        run,
        mesh=mesh,
        in_specs=(
            P("fsdp", None, "rep", "tp"),
            P(None, ("rep", "fsdp"), "tp"),
            P(None, ("rep", "fsdp"), "tp"),
            P(None, ("rep", "fsdp"), "tp"),
            P(("rep", "fsdp"), None, "tp"),
            P(("rep", "fsdp"), None, "tp"),
            P(("rep", "fsdp"), None, None, "tp"),
            P(("rep", "fsdp")),
        ),
        out_specs=(
            P(None, ("rep", "fsdp"), "tp"),
            P(None, ("rep", "fsdp"), "tp"),
            P(None, ("rep", "fsdp"), "tp"),
            P(("rep", "fsdp"), None, "tp"),
        ),
        check_vma=False,
    )
```

```python
import functools

import jax
import jax.numpy as jnp
from jax import lax
from jax.experimental import pallas as pl
from jax.experimental.pallas import tpu as pltpu
from jax.sharding import PartitionSpec as P

HD = 128
MESH = pl.DeviceIdType.MESH
W_CHUNKS = 4
ADAM_SUB = 32
TAIL_ROWS = 8


def learner_kernel(
    sizes, grad_hbm, master_hbm, one_hbm, two_hbm, x_hbm, kv_hbm,
    fresh_out, cached_out, master_out, one_out, two_out,
    own_grad, peer_grad, master, one, two, wbuf, xbuf, xflat, acc, partner_acc, kv_raw, kv_flat,
    local_sem, out_sem, grad_send, grad_recv, x_send, x_recv, x_swap_send,
    w_send, w_recv, w_fwd_send, acc_send, acc_recv,
):
    n_tp, depth = sizes
    r, f, t = lax.axis_index("rep"), lax.axis_index("fsdp"), lax.axis_index("tp")
    nf = 1 - f
    rx = r + 1 - 2 * lax.rem(r, 2)
    ry = lax.rem(r + 2, 4)
    rd = lax.rem(rx + 2, 4)
    partner, dev_x, dev_y = (r, nf, t), (rx, f, t), (ry, f, t)
    up, down = (r, f, t + 1), (r, f, t - 1)
    chunk = depth // W_CHUNKS

    def half(index):
        return pl.ds(pl.multiple_of(index * depth, depth), depth)

    local = [
        pltpu.make_async_copy(grad_hbm.at[0, :, half(f), :], own_grad, local_sem.at[0]),
        pltpu.make_async_copy(master_hbm, master, local_sem.at[1]),
        pltpu.make_async_copy(one_hbm, one, local_sem.at[2]),
        pltpu.make_async_copy(two_hbm, two, local_sem.at[3]),
        pltpu.make_async_copy(x_hbm.at[:, :, half(f)], xbuf.at[t, f], local_sem.at[4]),
        pltpu.make_async_copy(kv_hbm, kv_raw, local_sem.at[5]),
    ]
    for copy in local:
        copy.start()

    barrier = pltpu.get_barrier_semaphore()
    for device in (partner, dev_x, dev_y):
        pl.semaphore_signal(barrier, inc=1, device_id=device, device_id_type=MESH)

    @pl.when(t < n_tp - 1)
    def _():
        pl.semaphore_signal(barrier, inc=1, device_id=up, device_id_type=MESH)

    @pl.when(t > 0)
    def _():
        pl.semaphore_signal(barrier, inc=1, device_id=down, device_id_type=MESH)

    pl.semaphore_wait(barrier, jnp.where((t > 0) & (t < n_tp - 1), 5, 4))

    def rows(c):
        return pl.ds(pl.multiple_of(c * chunk, chunk), chunk)

    def remote(src, dst, send, recv, device):
        return pltpu.make_async_remote_copy(
            src_ref=src, dst_ref=dst, send_sem=send, recv_sem=recv,
            device_id=device, device_id_type=MESH,
        )

    def grad_copy(c):
        source = pl.ds(pl.multiple_of(nf * depth + c * chunk, chunk), chunk)
        return remote(
            grad_hbm.at[0, :, source, :], peer_grad.at[:, rows(c), :],
            grad_send.at[c], grad_recv.at[c], partner,
        )

    def x_move(z, th, side):
        return remote(
            xbuf.at[z, th], xbuf.at[z, th], x_send.at[side, z, th], x_recv.at[z, th],
            up if side == 1 else down,
        )

    def x_own(side):
        return remote(
            x_hbm.at[:, :, half(f)], xbuf.at[t, f], x_send.at[side, t, f], x_recv.at[t, f],
            up if side == 1 else down,
        )

    x_swap = remote(x_hbm.at[:, :, half(nf)], xbuf.at[t, f], x_swap_send.at[0], x_recv.at[t, f], partner)

    def both_ways(act):
        @pl.when(t < n_tp - 1)
        def _():
            act(1)

        @pl.when(t > 0)
        def _():
            act(0)

    grad_copy(0).start()
    x_swap.start()
    both_ways(lambda side: x_own(side).start())
    for c in range(1, W_CHUNKS):
        grad_copy(c).start()

    def w_copy(c, way):
        return remote(
            wbuf.at[r, :, rows(c), :], wbuf.at[r, :, rows(c), :],
            w_send.at[way, c], w_recv.at[r, c], dev_x if way == 0 else dev_y,
        )

    def w_arrived(owner, c):
        remote(
            wbuf.at[owner, :, rows(c), :], wbuf.at[owner, :, rows(c), :],
            w_send.at[0, c], w_recv.at[owner, c], dev_x,
        ).wait_recv()

    def w_forward(c):
        owner, device = (rx, dev_y) if c % 2 == 0 else (ry, dev_x)
        return remote(
            wbuf.at[owner, :, rows(c), :], wbuf.at[owner, :, rows(c), :],
            w_fwd_send.at[c], w_recv.at[owner, c], device,
        )

    def x_arrived(z, th):
        x_move(z, th, 1).wait_recv()

    for copy in local[:4]:
        copy.wait()

    first_bias = 1.0 - 0.9**10
    second_bias = 1.0 - 0.95**10

    def adam(c):
        def sub(i, carry):
            at = pl.ds(pl.multiple_of(c * chunk + i * ADAM_SUB, ADAM_SUB), ADAM_SUB)
            gradient = own_grad[:, at, :].astype(jnp.float32) + peer_grad[:, at, :].astype(jnp.float32)
            new_one = 0.9 * one[:, at, :] + (1.0 - 0.9) * gradient
            new_two = 0.95 * two[:, at, :] + (1.0 - 0.95) * gradient * gradient
            update = new_one / first_bias / (jnp.sqrt(new_two / second_bias) + 1e-08)
            old = master[:, at, :]
            new_master = old - 0.001 * (update + 0.1 * old)
            one[:, at, :] = new_one
            two[:, at, :] = new_two
            master[:, at, :] = new_master
            wbuf[r, :, at, :] = new_master.astype(jnp.bfloat16)
            return carry

        lax.fori_loop(0, chunk // ADAM_SUB, sub, 0)

    for c in range(W_CHUNKS):
        grad_copy(c).wait_recv()
        adam(c)
        if c == 0:
            x_arrived(t, nf)
            both_ways(lambda side: x_move(t, nf, side).start())
        else:
            w_copy(c - 1, 0).start()
            w_copy(c - 1, 1).start()
    outs = [
        pltpu.make_async_copy(master, master_out, out_sem.at[0]),
        pltpu.make_async_copy(one, one_out, out_sem.at[1]),
        pltpu.make_async_copy(two, two_out, out_sem.at[2]),
    ]
    for copy in outs:
        copy.start()
    w_copy(W_CHUNKS - 1, 0).start()
    w_copy(W_CHUNKS - 1, 1).start()
    local[4].wait()
    local[5].wait()

    def x_step(k, th):
        @pl.when(t - k >= 0)
        def _():
            x_arrived(t - k, th)

            @pl.when(t < n_tp - 1)
            def _():
                x_move(t - k, th, 1).start()

        @pl.when(t + k < n_tp)
        def _():
            x_arrived(t + k, th)

            @pl.when(t > 0)
            def _():
                x_move(t + k, th, 0).start()

    def w_step(c):
        w_arrived(rx, c)
        w_arrived(ry, c)
        w_forward(c).start()

    kv_rows, cache_len = kv_raw.shape[:2]
    pieces = kv_rows // 8

    def split_cache(quarter):
        def body(i, carry):
            row = (quarter * pieces + i) * 2
            at = pl.ds(pl.multiple_of(row * cache_len, 2 * cache_len), 2 * cache_len)
            for j in range(2):
                kv_flat[j, at, :] = kv_raw[pl.ds(row, 2), :, j, :].reshape(2 * cache_len, -1)
            return carry

        lax.fori_loop(0, pieces, body, 0)

    split_cache(0)
    x_step(1, f)
    split_cache(1)
    w_step(0)
    split_cache(2)
    x_step(1, nf)
    split_cache(3)
    cached_copy = pltpu.make_async_copy(kv_flat, cached_out, out_sem.at[3])
    cached_copy.start()
    w_step(1)
    w_step(2)
    x_step(2, f)
    w_step(3)
    x_step(2, nf)

    acc[...] = jnp.zeros_like(acc)

    x_rows = xbuf.shape[2]
    x_part = x_rows // 4
    flat_part = xflat.shape[0] // 4

    def multiply(z, th):
        def flatten(i, carry):
            at = pl.ds(pl.multiple_of(i * flat_part, flat_part), flat_part)
            xflat[at, :] = xbuf[z, th, pl.ds(i * x_part, x_part)].reshape(flat_part, depth)
            return carry

        lax.fori_loop(0, 4, flatten, 0)

        def one_side(kv, carry):
            acc[th, kv] += jnp.dot(xflat[...], wbuf[z, kv], preferred_element_type=jnp.float32)
            return carry

        lax.fori_loop(0, 2, one_side, 0)

    for c in range(W_CHUNKS):
        w_arrived(rd, c)

    def step(j, carry):
        k = j // 2
        th = f + lax.rem(j, 2) * (1 - 2 * f)

        def side(s, inner):
            z = t + (2 * s - 1) * k

            @pl.when((z >= 0) & (z < n_tp))
            def _():
                @pl.when(k == n_tp - 1)
                def _():
                    x_arrived(z, th)

                multiply(z, th)

            return inner

        lax.fori_loop(jnp.where(k == 0, 1, 0), 2, side, 0)
        return carry

    lax.fori_loop(0, 2 * n_tp, step, 0)

    swap = remote(acc.at[nf], partner_acc, acc_send.at[0], acc_recv.at[0], partner)
    swap.start()
    for c in range(W_CHUNKS):
        grad_copy(c).wait_send()
        w_copy(c, 0).wait_send()
        w_copy(c, 1).wait_send()
        w_forward(c).wait_send()
    x_swap.wait_send()
    both_ways(lambda side: x_own(side).wait_send())
    both_ways(lambda side: x_move(t, nf, side).wait_send())
    for k in range(1, n_tp - 1):
        for th in (f, nf):
            @pl.when((t - k >= 0) & (t < n_tp - 1))
            def _():
                x_move(t - k, th, 1).wait_send()

            @pl.when((t + k < n_tp) & (t > 0))
            def _():
                x_move(t + k, th, 0).wait_send()
    for copy in outs:
        copy.wait()
    cached_copy.wait()
    swap.wait_recv()
    fresh_out[...] = (acc[f] + partner_acc[...]).astype(jnp.bfloat16)
    swap.wait_send()


def tail_kernel(
    lengths, q_ref, kv_ref, fresh_in, master_in, one_in, two_in,
    context, master_out, one_out, two_out, fresh_ref, sem,
):
    block = pl.program_id(0)
    moves = [
        pltpu.make_async_copy(master_in, master_out, sem.at[1]),
        pltpu.make_async_copy(one_in, one_out, sem.at[2]),
        pltpu.make_async_copy(two_in, two_out, sem.at[3]),
    ]

    @pl.when(block == 0)
    def _():
        fresh_copy = pltpu.make_async_copy(fresh_in, fresh_ref, sem.at[0])
        fresh_copy.start()
        for move in moves:
            move.start()
        fresh_copy.wait()

    row_count, step_count, features = q_ref.shape
    cached = kv_ref.shape[1]
    head = HD
    cache_len = cached // row_count
    tokens = row_count * step_count
    keys = cached + tokens
    groups = fresh_ref.shape[2] // head
    per_group = features // head // groups
    here = pl.ds(pl.multiple_of(block * tokens, tokens), tokens)
    column = lax.broadcasted_iota(jnp.int32, (1, keys), 1)
    is_old = column < cached
    new_column = column - cached
    key_row = jnp.where(is_old, column // cache_len, new_column // step_count)
    position = column - key_row * cache_len
    limit = jnp.zeros((1, keys), jnp.int32)
    for row in range(row_count):
        limit = jnp.where(key_row == row, lengths[block * row_count + row], limit)
    old_row = jnp.where(is_old & (position < limit), key_row, -1)
    new_row = jnp.where(is_old, -1, key_row)
    token = lax.broadcasted_iota(jnp.int32, (tokens, 1), 0)
    row = token // step_count
    valid = (old_row == row) | ((new_row == row) & (new_column <= token))
    low = -0.7 * float(jnp.finfo(jnp.float32).max)
    contract = (((1,), (1,)), ((), ()))
    for group in range(groups):
        cols = slice(group * head, (group + 1) * head)
        query = jnp.concatenate(
            [
                q_ref[:, :, (group * per_group + h) * head : (group * per_group + h + 1) * head].reshape(tokens, head)
                for h in range(per_group)
            ],
            axis=0,
        )
        key = jnp.concatenate([kv_ref[0, :, cols], fresh_ref[0, here, cols]], axis=0)
        value = jnp.concatenate([kv_ref[1, :, cols], fresh_ref[1, here, cols]], axis=0)
        scores = lax.dot_general(query, key, contract, preferred_element_type=jnp.float32)
        scores = jnp.where(valid[None], scores.reshape(per_group, tokens, keys) * head**-0.5, low)
        weights = jnp.exp(scores - jnp.max(scores, axis=-1, keepdims=True))
        weights = weights * (1.0 / jnp.sum(weights, axis=-1, keepdims=True))
        weights = weights.astype(jnp.bfloat16).reshape(per_group * tokens, keys)
        out = jnp.dot(weights, value, preferred_element_type=jnp.float32)
        for h in range(per_group):
            at = (group * per_group + h) * head
            piece = out[h * tokens : (h + 1) * tokens].reshape(row_count, step_count, head)
            context[:, :, at : at + head] = piece.astype(jnp.bfloat16)

    @pl.when(block == pl.num_programs(0) - 1)
    def _():
        for move in moves:
            move.wait()


def fused_device(n_rep, grad_parts, master_weight, moment_one, moment_two, layer_inputs, queries, kv_cache, lengths):
    row_count, step_count, features = layer_inputs.shape
    _, depth, width = master_weight.shape
    n_tp = n_rep
    tokens = row_count * step_count
    cache_len = kv_cache.shape[1]
    bf16, f32 = jnp.bfloat16, jnp.float32
    dma = pltpu.SemaphoreType.DMA
    state = jax.ShapeDtypeStruct(master_weight.shape, f32)
    any_spec = pl.BlockSpec(memory_space=pl.ANY)
    hbm_spec = pl.BlockSpec(memory_space=pltpu.HBM)
    in_place = [
        pltpu.with_memory_space_constraint(array, pltpu.HBM)
        for array in (grad_parts, master_weight, moment_one, moment_two, layer_inputs, kv_cache)
    ]
    fresh, cached, master, one, two = pl.pallas_call(
        functools.partial(learner_kernel, (n_tp, depth)),
        out_shape=(
            jax.ShapeDtypeStruct((2, tokens, width), bf16),
            jax.ShapeDtypeStruct((2, row_count * cache_len, width), bf16),
            state,
            state,
            state,
        ),
        in_specs=[hbm_spec] * 6,
        out_specs=(pl.BlockSpec(memory_space=pltpu.VMEM), hbm_spec, any_spec, any_spec, any_spec),
        scratch_shapes=[
            pltpu.VMEM((2, depth, width), bf16),
            pltpu.VMEM((2, depth, width), bf16),
            pltpu.VMEM((2, depth, width), f32),
            pltpu.VMEM((2, depth, width), f32),
            pltpu.VMEM((2, depth, width), f32),
            pltpu.VMEM((n_rep, 2, depth, width), bf16),
            pltpu.VMEM((n_tp, 2, row_count, step_count, depth), bf16),
            pltpu.VMEM((tokens, depth), bf16),
            pltpu.VMEM((2, 2, tokens, width), f32),
            pltpu.VMEM((2, tokens, width), f32),
            pltpu.VMEM(kv_cache.shape, bf16),
            pltpu.VMEM((2, row_count * cache_len, width), bf16),
            dma((6,)),
            dma((4,)),
            dma((W_CHUNKS,)),
            dma((W_CHUNKS,)),
            dma((2, n_tp, 2)),
            dma((n_tp, 2)),
            dma((1,)),
            dma((2, W_CHUNKS)),
            dma((n_rep, W_CHUNKS)),
            dma((W_CHUNKS,)),
            dma((1,)),
            dma((1,)),
        ],
        compiler_params=pltpu.CompilerParams(
            collective_id=0, has_side_effects=True, vmem_limit_bytes=36 * 1024 * 1024
        ),
    )(*in_place)
    token_spec = pl.BlockSpec((TAIL_ROWS, step_count, features), lambda i, *_: (i, 0, 0))
    context, master, one, two = pl.pallas_call(
        tail_kernel,
        out_shape=(jax.ShapeDtypeStruct(queries.shape, bf16), state, state, state),
        grid_spec=pltpu.PrefetchScalarGridSpec(
            num_scalar_prefetch=1,
            grid=(row_count // TAIL_ROWS,),
            in_specs=[
                token_spec,
                pl.BlockSpec((2, TAIL_ROWS * cache_len, width), lambda i, *_: (0, i, 0)),
                any_spec,
                any_spec,
                any_spec,
                any_spec,
            ],
            out_specs=(token_spec, hbm_spec, hbm_spec, hbm_spec),
            scratch_shapes=[pltpu.VMEM((2, tokens, width), bf16), dma((4,))],
        ),
        compiler_params=pltpu.CompilerParams(
            dimension_semantics=("arbitrary",), vmem_limit_bytes=16 * 1024 * 1024
        ),
    )(lengths, queries, cached, fresh, master, one, two)
    return (master, one, two, context)


beta_one = 0.9
beta_two = 0.95
learning_rate = 0.001
weight_decay = 0.1
epsilon = 1e-08
first_bias = 1.0 - 0.9**10
second_bias = 1.0 - 0.95**10


def adamw_update(gradient, master, moment_one, moment_two):
    new_one = beta_one * moment_one + (1.0 - beta_one) * gradient
    new_two = beta_two * moment_two + (1.0 - beta_two) * gradient * gradient
    update = new_one / first_bias / (jnp.sqrt(new_two / second_bias) + epsilon)
    new_master = master - learning_rate * (update + weight_decay * master)
    return (new_one, new_two, new_master)


def attend(queries, kv_cache, fresh_keys, fresh_values, lengths):
    row_count = queries.shape[0]
    step_count = queries.shape[1]
    kv_heads = fresh_keys.shape[2]
    cache_len = kv_cache.shape[1]
    grouped = queries.reshape(row_count, step_count, kv_heads, -1, HD)
    cached_keys = kv_cache[:, :, 0].reshape(row_count, cache_len, kv_heads, HD)
    cached_values = kv_cache[:, :, 1].reshape(row_count, cache_len, kv_heads, HD)
    scaling = 1.0 / jnp.sqrt(jnp.float32(HD))
    cached_scores = (
        jnp.einsum("rsgqd,rcgd->rsgqc", grouped, cached_keys, preferred_element_type=jnp.float32)
        * scaling
    )
    fresh_scores = (
        jnp.einsum("rsgqd,rugd->rsgqu", grouped, fresh_keys, preferred_element_type=jnp.float32)
        * scaling
    )
    valid_old = jnp.arange(cache_len, dtype=jnp.int32)[None, :] < lengths[:, None]
    valid_old = valid_old[:, None, None, None, :]
    steps_index = jnp.arange(step_count, dtype=jnp.int32)
    valid_new = (steps_index[None, :] <= steps_index[:, None])[None, :, None, None, :]
    scores = jnp.concatenate(
        [
            jnp.where(valid_old, cached_scores, -jnp.inf),
            jnp.where(valid_new, fresh_scores, -jnp.inf),
        ],
        axis=-1,
    )
    row_max = jnp.max(scores, axis=-1, keepdims=True)
    exponent = jnp.exp(scores - row_max)
    weights = (exponent / jnp.sum(exponent, axis=-1, keepdims=True)).astype(jnp.bfloat16)
    output = jnp.einsum(
        "rsgqc,rcgd->rsgqd",
        weights[..., :cache_len],
        cached_values,
        preferred_element_type=jnp.float32,
    )
    output = output + jnp.einsum(
        "rsgqu,rugd->rsgqd",
        weights[..., cache_len:],
        fresh_values,
        preferred_element_type=jnp.float32,
    )
    return output.astype(jnp.bfloat16).reshape(row_count, step_count, -1)


def on_device(
    grad_parts, master_weight, moment_one, moment_two, layer_inputs, queries, kv_cache, lengths
):
    gradient = lax.psum_scatter(
        grad_parts[0].astype(jnp.float32).astype(jnp.bfloat16),
        "fsdp",
        scatter_dimension=1,
        tiled=True,
    ).astype(jnp.float32)
    new_one, new_two, new_master = adamw_update(gradient, master_weight, moment_one, moment_two)
    rollout_weight = new_master.astype(jnp.bfloat16)
    row_count = layer_inputs.shape[0]
    step_count = layer_inputs.shape[1]
    gathered = lax.all_gather(layer_inputs, "tp", axis=2, tiled=True)
    flattened = gathered.reshape(row_count * step_count, gathered.shape[2])
    projected = jnp.einsum(
        "td,kdc->ktc",
        flattened,
        lax.all_gather(rollout_weight, ("rep", "fsdp"), axis=1, tiled=True),
        preferred_element_type=jnp.float32,
    )
    fresh_pair = projected.astype(jnp.bfloat16).reshape(2, row_count, step_count, -1, HD)
    context = attend(queries, kv_cache, fresh_pair[0], fresh_pair[1], lengths)
    return (new_master, new_one, new_two, context)


def solution(mesh):
    shape = mesh.shape
    fits = shape["rep"] == 4 and shape["tp"] == 4 and shape["fsdp"] == 2
    run = functools.partial(fused_device, shape["rep"]) if fits else on_device
    return jax.shard_map(
        run,
        mesh=mesh,
        in_specs=(
            P("fsdp", None, "rep", "tp"),
            P(None, ("rep", "fsdp"), "tp"),
            P(None, ("rep", "fsdp"), "tp"),
            P(None, ("rep", "fsdp"), "tp"),
            P(("rep", "fsdp"), None, "tp"),
            P(("rep", "fsdp"), None, "tp"),
            P(("rep", "fsdp"), None, None, "tp"),
            P(("rep", "fsdp")),
        ),
        out_specs=(
            P(None, ("rep", "fsdp"), "tp"),
            P(None, ("rep", "fsdp"), "tp"),
            P(None, ("rep", "fsdp"), "tp"),
            P(("rep", "fsdp"), None, "tp"),
        ),
        check_vma=False,
    )
```

```python
import functools

import jax
import jax.numpy as jnp
from jax import lax
from jax.experimental import pallas as pl
from jax.experimental.pallas import tpu as pltpu
from jax.sharding import PartitionSpec as P

HD = 128
MESH = pl.DeviceIdType.MESH
W_CHUNKS = 4
ADAM_SUB = 32
TAIL_ROWS = 8


def learner_kernel(
    sizes, grad_hbm, master_hbm, one_hbm, two_hbm, x_hbm, kv_hbm,
    fresh_out, cached_out, master_out, one_out, two_out,
    own_grad, peer_grad, master, one, two, wbuf, xbuf, xflat, acc, partner_acc, kv_raw, kv_flat,
    local_sem, out_sem, grad_send, grad_recv, x_send, x_recv, x_swap_send,
    w_send, w_recv, w_fwd_send, acc_send, acc_recv,
):
    n_tp, depth = sizes
    r, f, t = lax.axis_index("rep"), lax.axis_index("fsdp"), lax.axis_index("tp")
    nf = 1 - f
    rx = r + 1 - 2 * lax.rem(r, 2)
    ry = lax.rem(r + 2, 4)
    rd = lax.rem(rx + 2, 4)
    partner, dev_x, dev_y = (r, nf, t), (rx, f, t), (ry, f, t)
    up, down = (r, f, t + 1), (r, f, t - 1)
    chunk = depth // W_CHUNKS

    def half(index):
        return pl.ds(pl.multiple_of(index * depth, depth), depth)

    local = [
        pltpu.make_async_copy(grad_hbm.at[0, :, half(f), :], own_grad, local_sem.at[0]),
        pltpu.make_async_copy(master_hbm, master, local_sem.at[1]),
        pltpu.make_async_copy(one_hbm, one, local_sem.at[2]),
        pltpu.make_async_copy(two_hbm, two, local_sem.at[3]),
        pltpu.make_async_copy(x_hbm.at[:, :, half(f)], xbuf.at[t, f], local_sem.at[4]),
        pltpu.make_async_copy(kv_hbm, kv_raw, local_sem.at[5]),
    ]
    for copy in local:
        copy.start()

    barrier = pltpu.get_barrier_semaphore()
    for device in (partner, dev_x, dev_y):
        pl.semaphore_signal(barrier, inc=1, device_id=device, device_id_type=MESH)

    @pl.when(t < n_tp - 1)
    def _():
        pl.semaphore_signal(barrier, inc=1, device_id=up, device_id_type=MESH)

    @pl.when(t > 0)
    def _():
        pl.semaphore_signal(barrier, inc=1, device_id=down, device_id_type=MESH)

    pl.semaphore_wait(barrier, jnp.where((t > 0) & (t < n_tp - 1), 5, 4))

    def rows(c):
        return pl.ds(pl.multiple_of(c * chunk, chunk), chunk)

    def remote(src, dst, send, recv, device):
        return pltpu.make_async_remote_copy(
            src_ref=src, dst_ref=dst, send_sem=send, recv_sem=recv,
            device_id=device, device_id_type=MESH,
        )

    def grad_copy(c):
        source = pl.ds(pl.multiple_of(nf * depth + c * chunk, chunk), chunk)
        return remote(
            grad_hbm.at[0, :, source, :], peer_grad.at[:, rows(c), :],
            grad_send.at[c], grad_recv.at[c], partner,
        )

    def x_move(z, th, side):
        return remote(
            xbuf.at[z, th], xbuf.at[z, th], x_send.at[side, z, th], x_recv.at[z, th],
            up if side == 1 else down,
        )

    def x_own(side):
        return remote(
            x_hbm.at[:, :, half(f)], xbuf.at[t, f], x_send.at[side, t, f], x_recv.at[t, f],
            up if side == 1 else down,
        )

    x_swap = remote(x_hbm.at[:, :, half(nf)], xbuf.at[t, f], x_swap_send.at[0], x_recv.at[t, f], partner)

    def both_ways(act):
        @pl.when(t < n_tp - 1)
        def _():
            act(1)

        @pl.when(t > 0)
        def _():
            act(0)

    grad_copy(0).start()
    x_swap.start()
    both_ways(lambda side: x_own(side).start())
    for c in range(1, W_CHUNKS):
        grad_copy(c).start()

    def w_copy(c, way):
        return remote(
            wbuf.at[r, :, rows(c), :], wbuf.at[r, :, rows(c), :],
            w_send.at[way, c], w_recv.at[r, c], dev_x if way == 0 else dev_y,
        )

    def w_arrived(owner, c):
        remote(
            wbuf.at[owner, :, rows(c), :], wbuf.at[owner, :, rows(c), :],
            w_send.at[0, c], w_recv.at[owner, c], dev_x,
        ).wait_recv()

    def w_forward(c):
        owner, device = (rx, dev_y) if c % 2 == 0 else (ry, dev_x)
        return remote(
            wbuf.at[owner, :, rows(c), :], wbuf.at[owner, :, rows(c), :],
            w_fwd_send.at[c], w_recv.at[owner, c], device,
        )

    def x_arrived(z, th):
        x_move(z, th, 1).wait_recv()

    for copy in local[:4]:
        copy.wait()

    first_bias = 1.0 - 0.9**10
    second_bias = 1.0 - 0.95**10

    def adam(c):
        def sub(i, carry):
            at = pl.ds(pl.multiple_of(c * chunk + i * ADAM_SUB, ADAM_SUB), ADAM_SUB)
            gradient = own_grad[:, at, :].astype(jnp.float32) + peer_grad[:, at, :].astype(jnp.float32)
            new_one = 0.9 * one[:, at, :] + (1.0 - 0.9) * gradient
            new_two = 0.95 * two[:, at, :] + (1.0 - 0.95) * gradient * gradient
            update = new_one / first_bias / (jnp.sqrt(new_two / second_bias) + 1e-08)
            old = master[:, at, :]
            new_master = old - 0.001 * (update + 0.1 * old)
            one[:, at, :] = new_one
            two[:, at, :] = new_two
            master[:, at, :] = new_master
            wbuf[r, :, at, :] = new_master.astype(jnp.bfloat16)
            return carry

        lax.fori_loop(0, chunk // ADAM_SUB, sub, 0)

    for c in range(W_CHUNKS):
        grad_copy(c).wait_recv()
        adam(c)
        if c == 0:
            x_arrived(t, nf)
            both_ways(lambda side: x_move(t, nf, side).start())
        else:
            w_copy(c - 1, 0).start()
            w_copy(c - 1, 1).start()
    outs = [
        pltpu.make_async_copy(master, master_out, out_sem.at[0]),
        pltpu.make_async_copy(one, one_out, out_sem.at[1]),
        pltpu.make_async_copy(two, two_out, out_sem.at[2]),
    ]
    for copy in outs:
        copy.start()
    w_copy(W_CHUNKS - 1, 0).start()
    w_copy(W_CHUNKS - 1, 1).start()
    local[4].wait()
    local[5].wait()

    ends_up, ends_down = t + 1 == n_tp - 1, t == 1

    def x_wait(k, th):
        @pl.when(t - k >= 0)
        def _():
            x_arrived(t - k, th)

        @pl.when(t + k < n_tp)
        def _():
            x_arrived(t + k, th)

    def x_forward(k, th, go_up, go_down):
        @pl.when((t - k >= 0) & (t < n_tp - 1) & go_up)
        def _():
            x_move(t - k, th, 1).start()

        @pl.when((t + k < n_tp) & (t > 0) & go_down)
        def _():
            x_move(t + k, th, 0).start()

    def x_first_half():
        x_wait(1, f)
        x_forward(1, f, ends_up, ends_down)

    def x_second_half():
        x_wait(1, nf)
        x_forward(1, nf, True, True)
        x_forward(1, f, jnp.logical_not(ends_up), jnp.logical_not(ends_down))

    def x_far(k, th):
        x_wait(k, th)
        x_forward(k, th, True, True)

    def w_step(c):
        w_arrived(rx, c)
        w_arrived(ry, c)
        w_forward(c).start()

    kv_rows, cache_len = kv_raw.shape[:2]
    pieces = kv_rows // 8

    def split_cache(quarter):
        def body(i, carry):
            row = (quarter * pieces + i) * 2
            at = pl.ds(pl.multiple_of(row * cache_len, 2 * cache_len), 2 * cache_len)
            for j in range(2):
                kv_flat[j, at, :] = kv_raw[pl.ds(row, 2), :, j, :].reshape(2 * cache_len, -1)
            return carry

        lax.fori_loop(0, pieces, body, 0)

    split_cache(0)
    x_first_half()
    split_cache(1)
    w_step(0)
    split_cache(2)
    x_second_half()
    split_cache(3)
    cached_copy = pltpu.make_async_copy(kv_flat, cached_out, out_sem.at[3])
    cached_copy.start()
    w_step(1)
    w_step(2)
    x_far(2, nf)
    w_step(3)
    x_far(2, f)

    acc[...] = jnp.zeros_like(acc)

    x_rows = xbuf.shape[2]
    x_part = x_rows // 4
    flat_part = xflat.shape[0] // 4

    def multiply(z, th):
        def flatten(i, carry):
            at = pl.ds(pl.multiple_of(i * flat_part, flat_part), flat_part)
            xflat[at, :] = xbuf[z, th, pl.ds(i * x_part, x_part)].reshape(flat_part, depth)
            return carry

        lax.fori_loop(0, 4, flatten, 0)

        def one_side(kv, carry):
            acc[th, kv] += jnp.dot(xflat[...], wbuf[z, kv], preferred_element_type=jnp.float32)
            return carry

        lax.fori_loop(0, 2, one_side, 0)

    for c in range(W_CHUNKS):
        w_arrived(rd, c)

    def step(j, carry):
        k = j // 2
        th = nf + lax.rem(j, 2) * (1 - 2 * nf)

        def side(s, inner):
            z = t + (2 * s - 1) * k

            @pl.when((z >= 0) & (z < n_tp))
            def _():
                @pl.when(k == n_tp - 1)
                def _():
                    x_arrived(z, th)

                multiply(z, th)

            return inner

        lax.fori_loop(jnp.where(k == 0, 1, 0), 2, side, 0)
        return carry

    lax.fori_loop(0, 2 * n_tp - 1, step, 0)

    swap = remote(acc.at[nf], partner_acc, acc_send.at[0], acc_recv.at[0], partner)
    swap.start()
    step(2 * n_tp - 1, 0)
    for c in range(W_CHUNKS):
        grad_copy(c).wait_send()
        w_copy(c, 0).wait_send()
        w_copy(c, 1).wait_send()
        w_forward(c).wait_send()
    x_swap.wait_send()
    both_ways(lambda side: x_own(side).wait_send())
    both_ways(lambda side: x_move(t, nf, side).wait_send())
    for k in range(1, n_tp - 1):
        for th in (f, nf):
            @pl.when((t - k >= 0) & (t < n_tp - 1))
            def _():
                x_move(t - k, th, 1).wait_send()

            @pl.when((t + k < n_tp) & (t > 0))
            def _():
                x_move(t + k, th, 0).wait_send()
    for copy in outs:
        copy.wait()
    cached_copy.wait()
    swap.wait_recv()
    fresh_out[...] = (acc[f] + partner_acc[...]).astype(jnp.bfloat16)
    swap.wait_send()


def tail_kernel(
    lengths, q_ref, kv_ref, fresh_in, master_in, one_in, two_in,
    context, master_out, one_out, two_out, fresh_ref, sem,
):
    block = pl.program_id(0)
    moves = [
        pltpu.make_async_copy(master_in, master_out, sem.at[1]),
        pltpu.make_async_copy(one_in, one_out, sem.at[2]),
        pltpu.make_async_copy(two_in, two_out, sem.at[3]),
    ]

    @pl.when(block == 0)
    def _():
        fresh_copy = pltpu.make_async_copy(fresh_in, fresh_ref, sem.at[0])
        fresh_copy.start()
        for move in moves:
            move.start()
        fresh_copy.wait()

    row_count, step_count, features = q_ref.shape
    cached = kv_ref.shape[1]
    head = HD
    cache_len = cached // row_count
    tokens = row_count * step_count
    keys = cached + tokens
    groups = fresh_ref.shape[2] // head
    per_group = features // head // groups
    here = pl.ds(pl.multiple_of(block * tokens, tokens), tokens)
    column = lax.broadcasted_iota(jnp.int32, (1, keys), 1)
    is_old = column < cached
    new_column = column - cached
    key_row = jnp.where(is_old, column // cache_len, new_column // step_count)
    position = column - key_row * cache_len
    limit = jnp.zeros((1, keys), jnp.int32)
    for row in range(row_count):
        limit = jnp.where(key_row == row, lengths[block * row_count + row], limit)
    old_row = jnp.where(is_old & (position < limit), key_row, -1)
    new_row = jnp.where(is_old, -1, key_row)
    token = lax.broadcasted_iota(jnp.int32, (tokens, 1), 0)
    row = token // step_count
    valid = (old_row == row) | ((new_row == row) & (new_column <= token))
    low = -0.7 * float(jnp.finfo(jnp.float32).max)
    contract = (((1,), (1,)), ((), ()))
    for group in range(groups):
        cols = slice(group * head, (group + 1) * head)
        query = jnp.concatenate(
            [
                q_ref[:, :, (group * per_group + h) * head : (group * per_group + h + 1) * head].reshape(tokens, head)
                for h in range(per_group)
            ],
            axis=0,
        )
        key = jnp.concatenate([kv_ref[0, :, cols], fresh_ref[0, here, cols]], axis=0)
        value = jnp.concatenate([kv_ref[1, :, cols], fresh_ref[1, here, cols]], axis=0)
        scores = lax.dot_general(query, key, contract, preferred_element_type=jnp.float32)
        scores = jnp.where(valid[None], scores.reshape(per_group, tokens, keys) * head**-0.5, low)
        weights = jnp.exp(scores - jnp.max(scores, axis=-1, keepdims=True))
        weights = weights * (1.0 / jnp.sum(weights, axis=-1, keepdims=True))
        weights = weights.astype(jnp.bfloat16).reshape(per_group * tokens, keys)
        out = jnp.dot(weights, value, preferred_element_type=jnp.float32)
        for h in range(per_group):
            at = (group * per_group + h) * head
            piece = out[h * tokens : (h + 1) * tokens].reshape(row_count, step_count, head)
            context[:, :, at : at + head] = piece.astype(jnp.bfloat16)

    @pl.when(block == pl.num_programs(0) - 1)
    def _():
        for move in moves:
            move.wait()


def fused_device(n_rep, grad_parts, master_weight, moment_one, moment_two, layer_inputs, queries, kv_cache, lengths):
    row_count, step_count, features = layer_inputs.shape
    _, depth, width = master_weight.shape
    n_tp = n_rep
    tokens = row_count * step_count
    cache_len = kv_cache.shape[1]
    bf16, f32 = jnp.bfloat16, jnp.float32
    dma = pltpu.SemaphoreType.DMA
    state = jax.ShapeDtypeStruct(master_weight.shape, f32)
    any_spec = pl.BlockSpec(memory_space=pl.ANY)
    hbm_spec = pl.BlockSpec(memory_space=pltpu.HBM)
    in_place = [
        pltpu.with_memory_space_constraint(array, pltpu.HBM)
        for array in (grad_parts, master_weight, moment_one, moment_two, layer_inputs, kv_cache)
    ]
    fresh, cached, master, one, two = pl.pallas_call(
        functools.partial(learner_kernel, (n_tp, depth)),
        out_shape=(
            jax.ShapeDtypeStruct((2, tokens, width), bf16),
            jax.ShapeDtypeStruct((2, row_count * cache_len, width), bf16),
            state,
            state,
            state,
        ),
        in_specs=[hbm_spec] * 6,
        out_specs=(pl.BlockSpec(memory_space=pltpu.VMEM), hbm_spec, any_spec, any_spec, any_spec),
        scratch_shapes=[
            pltpu.VMEM((2, depth, width), bf16),
            pltpu.VMEM((2, depth, width), bf16),
            pltpu.VMEM((2, depth, width), f32),
            pltpu.VMEM((2, depth, width), f32),
            pltpu.VMEM((2, depth, width), f32),
            pltpu.VMEM((n_rep, 2, depth, width), bf16),
            pltpu.VMEM((n_tp, 2, row_count, step_count, depth), bf16),
            pltpu.VMEM((tokens, depth), bf16),
            pltpu.VMEM((2, 2, tokens, width), f32),
            pltpu.VMEM((2, tokens, width), f32),
            pltpu.VMEM(kv_cache.shape, bf16),
            pltpu.VMEM((2, row_count * cache_len, width), bf16),
            dma((6,)),
            dma((4,)),
            dma((W_CHUNKS,)),
            dma((W_CHUNKS,)),
            dma((2, n_tp, 2)),
            dma((n_tp, 2)),
            dma((1,)),
            dma((2, W_CHUNKS)),
            dma((n_rep, W_CHUNKS)),
            dma((W_CHUNKS,)),
            dma((1,)),
            dma((1,)),
        ],
        compiler_params=pltpu.CompilerParams(
            collective_id=0, has_side_effects=True, vmem_limit_bytes=36 * 1024 * 1024
        ),
    )(*in_place)
    token_spec = pl.BlockSpec((TAIL_ROWS, step_count, features), lambda i, *_: (i, 0, 0))
    context, master, one, two = pl.pallas_call(
        tail_kernel,
        out_shape=(jax.ShapeDtypeStruct(queries.shape, bf16), state, state, state),
        grid_spec=pltpu.PrefetchScalarGridSpec(
            num_scalar_prefetch=1,
            grid=(row_count // TAIL_ROWS,),
            in_specs=[
                token_spec,
                pl.BlockSpec((2, TAIL_ROWS * cache_len, width), lambda i, *_: (0, i, 0)),
                any_spec,
                any_spec,
                any_spec,
                any_spec,
            ],
            out_specs=(token_spec, hbm_spec, hbm_spec, hbm_spec),
            scratch_shapes=[pltpu.VMEM((2, tokens, width), bf16), dma((4,))],
        ),
        compiler_params=pltpu.CompilerParams(
            dimension_semantics=("arbitrary",), vmem_limit_bytes=16 * 1024 * 1024
        ),
    )(lengths, queries, cached, fresh, master, one, two)
    return (master, one, two, context)


beta_one = 0.9
beta_two = 0.95
learning_rate = 0.001
weight_decay = 0.1
epsilon = 1e-08
first_bias = 1.0 - 0.9**10
second_bias = 1.0 - 0.95**10


def adamw_update(gradient, master, moment_one, moment_two):
    new_one = beta_one * moment_one + (1.0 - beta_one) * gradient
    new_two = beta_two * moment_two + (1.0 - beta_two) * gradient * gradient
    update = new_one / first_bias / (jnp.sqrt(new_two / second_bias) + epsilon)
    new_master = master - learning_rate * (update + weight_decay * master)
    return (new_one, new_two, new_master)


def attend(queries, kv_cache, fresh_keys, fresh_values, lengths):
    row_count = queries.shape[0]
    step_count = queries.shape[1]
    kv_heads = fresh_keys.shape[2]
    cache_len = kv_cache.shape[1]
    grouped = queries.reshape(row_count, step_count, kv_heads, -1, HD)
    cached_keys = kv_cache[:, :, 0].reshape(row_count, cache_len, kv_heads, HD)
    cached_values = kv_cache[:, :, 1].reshape(row_count, cache_len, kv_heads, HD)
    scaling = 1.0 / jnp.sqrt(jnp.float32(HD))
    cached_scores = (
        jnp.einsum("rsgqd,rcgd->rsgqc", grouped, cached_keys, preferred_element_type=jnp.float32)
        * scaling
    )
    fresh_scores = (
        jnp.einsum("rsgqd,rugd->rsgqu", grouped, fresh_keys, preferred_element_type=jnp.float32)
        * scaling
    )
    valid_old = jnp.arange(cache_len, dtype=jnp.int32)[None, :] < lengths[:, None]
    valid_old = valid_old[:, None, None, None, :]
    steps_index = jnp.arange(step_count, dtype=jnp.int32)
    valid_new = (steps_index[None, :] <= steps_index[:, None])[None, :, None, None, :]
    scores = jnp.concatenate(
        [
            jnp.where(valid_old, cached_scores, -jnp.inf),
            jnp.where(valid_new, fresh_scores, -jnp.inf),
        ],
        axis=-1,
    )
    row_max = jnp.max(scores, axis=-1, keepdims=True)
    exponent = jnp.exp(scores - row_max)
    weights = (exponent / jnp.sum(exponent, axis=-1, keepdims=True)).astype(jnp.bfloat16)
    output = jnp.einsum(
        "rsgqc,rcgd->rsgqd",
        weights[..., :cache_len],
        cached_values,
        preferred_element_type=jnp.float32,
    )
    output = output + jnp.einsum(
        "rsgqu,rugd->rsgqd",
        weights[..., cache_len:],
        fresh_values,
        preferred_element_type=jnp.float32,
    )
    return output.astype(jnp.bfloat16).reshape(row_count, step_count, -1)


def on_device(
    grad_parts, master_weight, moment_one, moment_two, layer_inputs, queries, kv_cache, lengths
):
    gradient = lax.psum_scatter(
        grad_parts[0].astype(jnp.float32).astype(jnp.bfloat16),
        "fsdp",
        scatter_dimension=1,
        tiled=True,
    ).astype(jnp.float32)
    new_one, new_two, new_master = adamw_update(gradient, master_weight, moment_one, moment_two)
    rollout_weight = new_master.astype(jnp.bfloat16)
    row_count = layer_inputs.shape[0]
    step_count = layer_inputs.shape[1]
    gathered = lax.all_gather(layer_inputs, "tp", axis=2, tiled=True)
    flattened = gathered.reshape(row_count * step_count, gathered.shape[2])
    projected = jnp.einsum(
        "td,kdc->ktc",
        flattened,
        lax.all_gather(rollout_weight, ("rep", "fsdp"), axis=1, tiled=True),
        preferred_element_type=jnp.float32,
    )
    fresh_pair = projected.astype(jnp.bfloat16).reshape(2, row_count, step_count, -1, HD)
    context = attend(queries, kv_cache, fresh_pair[0], fresh_pair[1], lengths)
    return (new_master, new_one, new_two, context)


def solution(mesh):
    shape = mesh.shape
    fits = shape["rep"] == 4 and shape["tp"] == 4 and shape["fsdp"] == 2
    run = functools.partial(fused_device, shape["rep"]) if fits else on_device
    return jax.shard_map(
        run,
        mesh=mesh,
        in_specs=(
            P("fsdp", None, "rep", "tp"),
            P(None, ("rep", "fsdp"), "tp"),
            P(None, ("rep", "fsdp"), "tp"),
            P(None, ("rep", "fsdp"), "tp"),
            P(("rep", "fsdp"), None, "tp"),
            P(("rep", "fsdp"), None, "tp"),
            P(("rep", "fsdp"), None, None, "tp"),
            P(("rep", "fsdp")),
        ),
        out_specs=(
            P(None, ("rep", "fsdp"), "tp"),
            P(None, ("rep", "fsdp"), "tp"),
            P(None, ("rep", "fsdp"), "tp"),
            P(("rep", "fsdp"), None, "tp"),
        ),
        check_vma=False,
    )
```

```python
import functools

import jax
import jax.numpy as jnp
from jax import lax
from jax.experimental import pallas as pl
from jax.experimental.pallas import tpu as pltpu
from jax.sharding import PartitionSpec as P

HD = 128
MESH = pl.DeviceIdType.MESH
W_CHUNKS = 4
ADAM_SUB = 32
TAIL_ROWS = 8
TAIL_BLOCKS = 3
LOG2E = 1.4426950408889634


def learner_kernel(
    sizes, grad_hbm, master_hbm, one_hbm, two_hbm, x_hbm, kv_hbm,
    fresh_out, cached_out, master_out, one_out, two_out,
    own_grad, peer_grad, master, one, two, wbuf, xbuf, xflat, acc, partner_acc, kv_raw, kv_flat,
    local_sem, out_sem, grad_send, grad_recv, x_send, x_recv, x_swap_send,
    w_send, w_recv, w_fwd_send, acc_send, acc_recv,
):
    n_tp, depth = sizes
    r, f, t = lax.axis_index("rep"), lax.axis_index("fsdp"), lax.axis_index("tp")
    nf = 1 - f
    rx = r + 1 - 2 * lax.rem(r, 2)
    ry = lax.rem(r + 2, 4)
    rd = lax.rem(rx + 2, 4)
    partner, dev_x, dev_y = (r, nf, t), (rx, f, t), (ry, f, t)
    up, down = (r, f, t + 1), (r, f, t - 1)
    chunk = depth // W_CHUNKS

    def half(index):
        return pl.ds(pl.multiple_of(index * depth, depth), depth)

    local = [
        pltpu.make_async_copy(grad_hbm.at[0, :, half(f), :], own_grad, local_sem.at[0]),
        pltpu.make_async_copy(master_hbm, master, local_sem.at[1]),
        pltpu.make_async_copy(one_hbm, one, local_sem.at[2]),
        pltpu.make_async_copy(two_hbm, two, local_sem.at[3]),
        pltpu.make_async_copy(x_hbm.at[:, :, half(f)], xbuf.at[t, f], local_sem.at[4]),
        pltpu.make_async_copy(kv_hbm, kv_raw, local_sem.at[5]),
    ]
    for copy in local:
        copy.start()

    barrier = pltpu.get_barrier_semaphore()
    for device in (partner, dev_x, dev_y):
        pl.semaphore_signal(barrier, inc=1, device_id=device, device_id_type=MESH)

    @pl.when(t < n_tp - 1)
    def _():
        pl.semaphore_signal(barrier, inc=1, device_id=up, device_id_type=MESH)

    @pl.when(t > 0)
    def _():
        pl.semaphore_signal(barrier, inc=1, device_id=down, device_id_type=MESH)

    pl.semaphore_wait(barrier, jnp.where((t > 0) & (t < n_tp - 1), 5, 4))

    def rows(c):
        return pl.ds(pl.multiple_of(c * chunk, chunk), chunk)

    def remote(src, dst, send, recv, device):
        return pltpu.make_async_remote_copy(
            src_ref=src, dst_ref=dst, send_sem=send, recv_sem=recv,
            device_id=device, device_id_type=MESH,
        )

    def grad_copy(c):
        source = pl.ds(pl.multiple_of(nf * depth + c * chunk, chunk), chunk)
        return remote(
            grad_hbm.at[0, :, source, :], peer_grad.at[:, rows(c), :],
            grad_send.at[c], grad_recv.at[c], partner,
        )

    def x_move(z, th, side):
        return remote(
            xbuf.at[z, th], xbuf.at[z, th], x_send.at[side, z, th], x_recv.at[z, th],
            up if side == 1 else down,
        )

    def x_own(side):
        return remote(
            x_hbm.at[:, :, half(f)], xbuf.at[t, f], x_send.at[side, t, f], x_recv.at[t, f],
            up if side == 1 else down,
        )

    x_swap = remote(x_hbm.at[:, :, half(nf)], xbuf.at[t, f], x_swap_send.at[0], x_recv.at[t, f], partner)

    def both_ways(act):
        @pl.when(t < n_tp - 1)
        def _():
            act(1)

        @pl.when(t > 0)
        def _():
            act(0)

    grad_copy(0).start()
    x_swap.start()
    both_ways(lambda side: x_own(side).start())
    for c in range(1, W_CHUNKS):
        grad_copy(c).start()

    def w_copy(c, way):
        return remote(
            wbuf.at[r, :, rows(c), :], wbuf.at[r, :, rows(c), :],
            w_send.at[way, c], w_recv.at[r, c], dev_x if way == 0 else dev_y,
        )

    def w_arrived(owner, c):
        remote(
            wbuf.at[owner, :, rows(c), :], wbuf.at[owner, :, rows(c), :],
            w_send.at[0, c], w_recv.at[owner, c], dev_x,
        ).wait_recv()

    def w_forward(c):
        owner, device = (rx, dev_y) if c % 2 == 0 else (ry, dev_x)
        return remote(
            wbuf.at[owner, :, rows(c), :], wbuf.at[owner, :, rows(c), :],
            w_fwd_send.at[c], w_recv.at[owner, c], device,
        )

    def x_arrived(z, th):
        x_move(z, th, 1).wait_recv()

    for copy in local[:4]:
        copy.wait()

    first_bias = 1.0 - 0.9**10
    second_bias = 1.0 - 0.95**10

    def adam(c):
        def sub(i, carry):
            at = pl.ds(pl.multiple_of(c * chunk + i * ADAM_SUB, ADAM_SUB), ADAM_SUB)
            gradient = own_grad[:, at, :].astype(jnp.float32) + peer_grad[:, at, :].astype(jnp.float32)
            new_one = 0.9 * one[:, at, :] + (1.0 - 0.9) * gradient
            new_two = 0.95 * two[:, at, :] + (1.0 - 0.95) * gradient * gradient
            update = new_one / first_bias / (jnp.sqrt(new_two / second_bias) + 1e-08)
            old = master[:, at, :]
            new_master = old - 0.001 * (update + 0.1 * old)
            one[:, at, :] = new_one
            two[:, at, :] = new_two
            master[:, at, :] = new_master
            wbuf[r, :, at, :] = new_master.astype(jnp.bfloat16)
            return carry

        lax.fori_loop(0, chunk // ADAM_SUB, sub, 0)

    for c in range(W_CHUNKS):
        grad_copy(c).wait_recv()
        adam(c)
        if c == 0:
            x_arrived(t, nf)
            both_ways(lambda side: x_move(t, nf, side).start())
        else:
            w_copy(c - 1, 0).start()
            w_copy(c - 1, 1).start()
    outs = [
        pltpu.make_async_copy(master, master_out, out_sem.at[0]),
        pltpu.make_async_copy(one, one_out, out_sem.at[1]),
        pltpu.make_async_copy(two, two_out, out_sem.at[2]),
    ]
    for copy in outs:
        copy.start()
    w_copy(W_CHUNKS - 1, 0).start()
    w_copy(W_CHUNKS - 1, 1).start()
    local[4].wait()
    local[5].wait()

    ends_up, ends_down = t + 1 == n_tp - 1, t == 1

    def x_wait(k, th):
        @pl.when(t - k >= 0)
        def _():
            x_arrived(t - k, th)

        @pl.when(t + k < n_tp)
        def _():
            x_arrived(t + k, th)

    def x_forward(k, th, go_up, go_down):
        @pl.when((t - k >= 0) & (t < n_tp - 1) & go_up)
        def _():
            x_move(t - k, th, 1).start()

        @pl.when((t + k < n_tp) & (t > 0) & go_down)
        def _():
            x_move(t + k, th, 0).start()

    def x_first_half():
        x_wait(1, f)
        x_forward(1, f, ends_up, ends_down)

    def x_second_half():
        x_wait(1, nf)
        x_forward(1, nf, True, True)
        x_forward(1, f, jnp.logical_not(ends_up), jnp.logical_not(ends_down))

    def x_far(k, th):
        x_wait(k, th)
        x_forward(k, th, True, True)

    def w_step(c):
        w_arrived(rx, c)
        w_arrived(ry, c)
        w_forward(c).start()

    kv_rows, cache_len = kv_raw.shape[:2]
    pieces = kv_rows // 8

    def split_cache(quarter):
        def body(i, carry):
            row = (quarter * pieces + i) * 2
            at = pl.ds(pl.multiple_of(row * cache_len, 2 * cache_len), 2 * cache_len)
            for j in range(2):
                kv_flat[j, at, :] = kv_raw[pl.ds(row, 2), :, j, :].reshape(2 * cache_len, -1)
            return carry

        lax.fori_loop(0, pieces, body, 0)

    split_cache(0)
    x_first_half()
    split_cache(1)
    w_step(0)
    split_cache(2)
    x_second_half()
    split_cache(3)
    cached_copy = pltpu.make_async_copy(kv_flat, cached_out, out_sem.at[3])
    cached_copy.start()
    w_step(1)
    w_step(2)
    x_far(2, nf)
    w_step(3)
    x_far(2, f)

    acc[...] = jnp.zeros_like(acc)

    x_rows = xbuf.shape[2]
    x_part = x_rows // 4
    flat_part = xflat.shape[0] // 4

    def multiply(z, th):
        def flatten(i, carry):
            at = pl.ds(pl.multiple_of(i * flat_part, flat_part), flat_part)
            xflat[at, :] = xbuf[z, th, pl.ds(i * x_part, x_part)].reshape(flat_part, depth)
            return carry

        lax.fori_loop(0, 4, flatten, 0)

        def one_side(kv, carry):
            acc[th, kv] += jnp.dot(xflat[...], wbuf[z, kv], preferred_element_type=jnp.float32)
            return carry

        lax.fori_loop(0, 2, one_side, 0)

    for c in range(W_CHUNKS):
        w_arrived(rd, c)

    def step(j, carry):
        k = j // 2
        th = nf + lax.rem(j, 2) * (1 - 2 * nf)

        def side(s, inner):
            z = t + (2 * s - 1) * k

            @pl.when((z >= 0) & (z < n_tp))
            def _():
                @pl.when(k == n_tp - 1)
                def _():
                    x_arrived(z, th)

                multiply(z, th)

            return inner

        lax.fori_loop(jnp.where(k == 0, 1, 0), 2, side, 0)
        return carry

    lax.fori_loop(0, 2 * n_tp - 1, step, 0)

    swap = remote(acc.at[nf], partner_acc, acc_send.at[0], acc_recv.at[0], partner)
    swap.start()
    step(2 * n_tp - 1, 0)
    for c in range(W_CHUNKS):
        grad_copy(c).wait_send()
        w_copy(c, 0).wait_send()
        w_copy(c, 1).wait_send()
        w_forward(c).wait_send()
    x_swap.wait_send()
    both_ways(lambda side: x_own(side).wait_send())
    both_ways(lambda side: x_move(t, nf, side).wait_send())
    for k in range(1, n_tp - 1):
        for th in (f, nf):
            @pl.when((t - k >= 0) & (t < n_tp - 1))
            def _():
                x_move(t - k, th, 1).wait_send()

            @pl.when((t + k < n_tp) & (t > 0))
            def _():
                x_move(t + k, th, 0).wait_send()
    for copy in outs:
        copy.wait()
    cached_copy.wait()
    swap.wait_recv()
    fresh_out[...] = (acc[f] + partner_acc[...]).astype(jnp.bfloat16)
    swap.wait_send()


def tail_kernel(
    lengths, q_ref, kv_ref, fresh_in, master_in, one_in, two_in,
    context, master_out, one_out, two_out, fresh_ref, sem,
):
    block = pl.program_id(0)
    moves = [
        pltpu.make_async_copy(master_in, master_out, sem.at[1]),
        pltpu.make_async_copy(one_in, one_out, sem.at[2]),
        pltpu.make_async_copy(two_in, two_out, sem.at[3]),
    ]

    @pl.when(block == 0)
    def _():
        fresh_copy = pltpu.make_async_copy(fresh_in, fresh_ref, sem.at[0])
        fresh_copy.start()
        for move in moves:
            move.start()
        fresh_copy.wait()

    step_rows, step_count, features = q_ref.shape
    row_count = TAIL_ROWS
    head = HD
    cache_len = kv_ref.shape[1] // step_rows
    cached = row_count * cache_len
    tokens = row_count * step_count
    keys = cached + tokens
    groups = fresh_ref.shape[2] // head
    per_group = features // head // groups
    column = lax.broadcasted_iota(jnp.int32, (1, keys), 1)
    is_old = column < cached
    new_column = column - cached
    key_row = jnp.where(is_old, column // cache_len, new_column // step_count)
    position = column - key_row * cache_len
    new_row = jnp.where(is_old, -1, key_row)
    token = lax.broadcasted_iota(jnp.int32, (tokens, 1), 0)
    row = token // step_count
    new_valid = (new_row == row) & (new_column <= token)
    low = -0.7 * float(jnp.finfo(jnp.float32).max)
    factor = head**-0.5 * LOG2E
    contract = (((1,), (1,)), ((), ()))
    for part in range(step_rows // row_count):
        first_row = part * row_count
        start = block * step_rows + first_row
        limit = jnp.zeros((1, keys), jnp.int32)
        for at in range(row_count):
            limit = jnp.where(key_row == at, lengths[start + at], limit)
        valid = (jnp.where(is_old & (position < limit), key_row, -1) == row) | new_valid
        here = pl.ds(pl.multiple_of(start * step_count, tokens), tokens)
        old = slice(first_row * cache_len, first_row * cache_len + cached)
        mine = slice(first_row, first_row + row_count)
        for group in range(groups):
            cols = slice(group * head, (group + 1) * head)
            query = jnp.concatenate(
                [
                    q_ref[mine, :, (group * per_group + h) * head : (group * per_group + h + 1) * head].reshape(
                        tokens, head
                    )
                    for h in range(per_group)
                ],
                axis=0,
            )
            key = jnp.concatenate([kv_ref[0, old, cols], fresh_ref[0, here, cols]], axis=0)
            value = jnp.concatenate([kv_ref[1, old, cols], fresh_ref[1, here, cols]], axis=0)
            scores = lax.dot_general(query, key, contract, preferred_element_type=jnp.float32)
            scores = jnp.where(valid[None], scores.reshape(per_group, tokens, keys), low)
            weights = jnp.exp2((scores - jnp.max(scores, axis=-1, keepdims=True)) * factor)
            weights = weights * (1.0 / jnp.sum(weights, axis=-1, keepdims=True))
            weights = weights.astype(jnp.bfloat16).reshape(per_group * tokens, keys)
            out = jnp.dot(weights, value, preferred_element_type=jnp.float32)
            for h in range(per_group):
                at = (group * per_group + h) * head
                piece = out[h * tokens : (h + 1) * tokens].reshape(row_count, step_count, head)
                context[mine, :, at : at + head] = piece.astype(jnp.bfloat16)

    @pl.when(block == pl.num_programs(0) - 1)
    def _():
        for move in moves:
            move.wait()


def fused_device(n_rep, grad_parts, master_weight, moment_one, moment_two, layer_inputs, queries, kv_cache, lengths):
    row_count, step_count, features = layer_inputs.shape
    _, depth, width = master_weight.shape
    n_tp = n_rep
    tokens = row_count * step_count
    cache_len = kv_cache.shape[1]
    bf16, f32 = jnp.bfloat16, jnp.float32
    dma = pltpu.SemaphoreType.DMA
    state = jax.ShapeDtypeStruct(master_weight.shape, f32)
    any_spec = pl.BlockSpec(memory_space=pl.ANY)
    hbm_spec = pl.BlockSpec(memory_space=pltpu.HBM)
    in_place = [
        pltpu.with_memory_space_constraint(array, pltpu.HBM)
        for array in (grad_parts, master_weight, moment_one, moment_two, layer_inputs, kv_cache)
    ]
    fresh, cached, master, one, two = pl.pallas_call(
        functools.partial(learner_kernel, (n_tp, depth)),
        out_shape=(
            jax.ShapeDtypeStruct((2, tokens, width), bf16),
            jax.ShapeDtypeStruct((2, row_count * cache_len, width), bf16),
            state,
            state,
            state,
        ),
        in_specs=[hbm_spec] * 6,
        out_specs=(pl.BlockSpec(memory_space=pltpu.VMEM), hbm_spec, any_spec, any_spec, any_spec),
        scratch_shapes=[
            pltpu.VMEM((2, depth, width), bf16),
            pltpu.VMEM((2, depth, width), bf16),
            pltpu.VMEM((2, depth, width), f32),
            pltpu.VMEM((2, depth, width), f32),
            pltpu.VMEM((2, depth, width), f32),
            pltpu.VMEM((n_rep, 2, depth, width), bf16),
            pltpu.VMEM((n_tp, 2, row_count, step_count, depth), bf16),
            pltpu.VMEM((tokens, depth), bf16),
            pltpu.VMEM((2, 2, tokens, width), f32),
            pltpu.VMEM((2, tokens, width), f32),
            pltpu.VMEM(kv_cache.shape, bf16),
            pltpu.VMEM((2, row_count * cache_len, width), bf16),
            dma((6,)),
            dma((4,)),
            dma((W_CHUNKS,)),
            dma((W_CHUNKS,)),
            dma((2, n_tp, 2)),
            dma((n_tp, 2)),
            dma((1,)),
            dma((2, W_CHUNKS)),
            dma((n_rep, W_CHUNKS)),
            dma((W_CHUNKS,)),
            dma((1,)),
            dma((1,)),
        ],
        compiler_params=pltpu.CompilerParams(
            collective_id=0, has_side_effects=True, vmem_limit_bytes=36 * 1024 * 1024
        ),
    )(*in_place)
    step_rows = TAIL_ROWS * TAIL_BLOCKS
    token_spec = pl.BlockSpec((step_rows, step_count, features), lambda i, *_: (i, 0, 0))
    context, master, one, two = pl.pallas_call(
        tail_kernel,
        out_shape=(jax.ShapeDtypeStruct(queries.shape, bf16), state, state, state),
        grid_spec=pltpu.PrefetchScalarGridSpec(
            num_scalar_prefetch=1,
            grid=(row_count // step_rows,),
            in_specs=[
                token_spec,
                pl.BlockSpec((2, step_rows * cache_len, width), lambda i, *_: (0, i, 0)),
                any_spec,
                any_spec,
                any_spec,
                any_spec,
            ],
            out_specs=(token_spec, hbm_spec, hbm_spec, hbm_spec),
            scratch_shapes=[pltpu.VMEM((2, tokens, width), bf16), dma((4,))],
        ),
        compiler_params=pltpu.CompilerParams(
            dimension_semantics=("arbitrary",), vmem_limit_bytes=16 * 1024 * 1024
        ),
    )(lengths, queries, cached, fresh, master, one, two)
    return (master, one, two, context)


beta_one = 0.9
beta_two = 0.95
learning_rate = 0.001
weight_decay = 0.1
epsilon = 1e-08
first_bias = 1.0 - 0.9**10
second_bias = 1.0 - 0.95**10


def adamw_update(gradient, master, moment_one, moment_two):
    new_one = beta_one * moment_one + (1.0 - beta_one) * gradient
    new_two = beta_two * moment_two + (1.0 - beta_two) * gradient * gradient
    update = new_one / first_bias / (jnp.sqrt(new_two / second_bias) + epsilon)
    new_master = master - learning_rate * (update + weight_decay * master)
    return (new_one, new_two, new_master)


def attend(queries, kv_cache, fresh_keys, fresh_values, lengths):
    row_count = queries.shape[0]
    step_count = queries.shape[1]
    kv_heads = fresh_keys.shape[2]
    cache_len = kv_cache.shape[1]
    grouped = queries.reshape(row_count, step_count, kv_heads, -1, HD)
    cached_keys = kv_cache[:, :, 0].reshape(row_count, cache_len, kv_heads, HD)
    cached_values = kv_cache[:, :, 1].reshape(row_count, cache_len, kv_heads, HD)
    scaling = 1.0 / jnp.sqrt(jnp.float32(HD))
    cached_scores = (
        jnp.einsum("rsgqd,rcgd->rsgqc", grouped, cached_keys, preferred_element_type=jnp.float32)
        * scaling
    )
    fresh_scores = (
        jnp.einsum("rsgqd,rugd->rsgqu", grouped, fresh_keys, preferred_element_type=jnp.float32)
        * scaling
    )
    valid_old = jnp.arange(cache_len, dtype=jnp.int32)[None, :] < lengths[:, None]
    valid_old = valid_old[:, None, None, None, :]
    steps_index = jnp.arange(step_count, dtype=jnp.int32)
    valid_new = (steps_index[None, :] <= steps_index[:, None])[None, :, None, None, :]
    scores = jnp.concatenate(
        [
            jnp.where(valid_old, cached_scores, -jnp.inf),
            jnp.where(valid_new, fresh_scores, -jnp.inf),
        ],
        axis=-1,
    )
    row_max = jnp.max(scores, axis=-1, keepdims=True)
    exponent = jnp.exp(scores - row_max)
    weights = (exponent / jnp.sum(exponent, axis=-1, keepdims=True)).astype(jnp.bfloat16)
    output = jnp.einsum(
        "rsgqc,rcgd->rsgqd",
        weights[..., :cache_len],
        cached_values,
        preferred_element_type=jnp.float32,
    )
    output = output + jnp.einsum(
        "rsgqu,rugd->rsgqd",
        weights[..., cache_len:],
        fresh_values,
        preferred_element_type=jnp.float32,
    )
    return output.astype(jnp.bfloat16).reshape(row_count, step_count, -1)


def on_device(
    grad_parts, master_weight, moment_one, moment_two, layer_inputs, queries, kv_cache, lengths
):
    gradient = lax.psum_scatter(
        grad_parts[0].astype(jnp.float32).astype(jnp.bfloat16),
        "fsdp",
        scatter_dimension=1,
        tiled=True,
    ).astype(jnp.float32)
    new_one, new_two, new_master = adamw_update(gradient, master_weight, moment_one, moment_two)
    rollout_weight = new_master.astype(jnp.bfloat16)
    row_count = layer_inputs.shape[0]
    step_count = layer_inputs.shape[1]
    gathered = lax.all_gather(layer_inputs, "tp", axis=2, tiled=True)
    flattened = gathered.reshape(row_count * step_count, gathered.shape[2])
    projected = jnp.einsum(
        "td,kdc->ktc",
        flattened,
        lax.all_gather(rollout_weight, ("rep", "fsdp"), axis=1, tiled=True),
        preferred_element_type=jnp.float32,
    )
    fresh_pair = projected.astype(jnp.bfloat16).reshape(2, row_count, step_count, -1, HD)
    context = attend(queries, kv_cache, fresh_pair[0], fresh_pair[1], lengths)
    return (new_master, new_one, new_two, context)


def solution(mesh):
    shape = mesh.shape
    fits = shape["rep"] == 4 and shape["tp"] == 4 and shape["fsdp"] == 2
    run = functools.partial(fused_device, shape["rep"]) if fits else on_device
    return jax.shard_map(
        run,
        mesh=mesh,
        in_specs=(
            P("fsdp", None, "rep", "tp"),
            P(None, ("rep", "fsdp"), "tp"),
            P(None, ("rep", "fsdp"), "tp"),
            P(None, ("rep", "fsdp"), "tp"),
            P(("rep", "fsdp"), None, "tp"),
            P(("rep", "fsdp"), None, "tp"),
            P(("rep", "fsdp"), None, None, "tp"),
            P(("rep", "fsdp")),
        ),
        out_specs=(
            P(None, ("rep", "fsdp"), "tp"),
            P(None, ("rep", "fsdp"), "tp"),
            P(None, ("rep", "fsdp"), "tp"),
            P(("rep", "fsdp"), None, "tp"),
        ),
        check_vma=False,
    )
```

```python
import functools

import jax
import jax.numpy as jnp
from jax import lax
from jax.experimental import pallas as pl
from jax.experimental.pallas import tpu as pltpu
from jax.sharding import PartitionSpec as P

HD = 128
MESH = pl.DeviceIdType.MESH
W_CHUNKS = 4
ADAM_SUB = 32
TAIL_ROWS = 8
TAIL_BLOCKS = 3
LOG2E = 1.4426950408889634


def learner_kernel(
    sizes, grad_hbm, master_hbm, one_hbm, two_hbm, x_hbm, kv_hbm,
    fresh_out, cached_out, master_out, one_out, two_out,
    own_grad, peer_grad, master, one, two, wbuf, xbuf, xflat, acc, partner_acc, kv_raw, kv_flat,
    local_sem, out_sem, grad_send, grad_recv, x_send, x_recv, x_swap_send,
    w_send, w_recv, w_fwd_send, acc_send, acc_recv,
):
    n_tp, depth = sizes
    r, f, t = lax.axis_index("rep"), lax.axis_index("fsdp"), lax.axis_index("tp")
    nf = 1 - f
    rx = r + 1 - 2 * lax.rem(r, 2)
    ry = lax.rem(r + 2, 4)
    rd = lax.rem(rx + 2, 4)
    partner, dev_x, dev_y = (r, nf, t), (rx, f, t), (ry, f, t)
    up, down = (r, f, t + 1), (r, f, t - 1)
    chunk = depth // W_CHUNKS

    def half(index):
        return pl.ds(pl.multiple_of(index * depth, depth), depth)

    local = [
        pltpu.make_async_copy(grad_hbm.at[0, :, half(f), :], own_grad, local_sem.at[0]),
        pltpu.make_async_copy(master_hbm, master, local_sem.at[1]),
        pltpu.make_async_copy(one_hbm, one, local_sem.at[2]),
        pltpu.make_async_copy(two_hbm, two, local_sem.at[3]),
        pltpu.make_async_copy(x_hbm.at[:, :, half(f)], xbuf.at[t, f], local_sem.at[4]),
        pltpu.make_async_copy(kv_hbm, kv_raw, local_sem.at[5]),
    ]
    for copy in local:
        copy.start()

    barrier = pltpu.get_barrier_semaphore()
    for device in (partner, dev_x, dev_y):
        pl.semaphore_signal(barrier, inc=1, device_id=device, device_id_type=MESH)

    @pl.when(t < n_tp - 1)
    def _():
        pl.semaphore_signal(barrier, inc=1, device_id=up, device_id_type=MESH)

    @pl.when(t > 0)
    def _():
        pl.semaphore_signal(barrier, inc=1, device_id=down, device_id_type=MESH)

    pl.semaphore_wait(barrier, jnp.where((t > 0) & (t < n_tp - 1), 5, 4))

    def rows(c):
        return pl.ds(pl.multiple_of(c * chunk, chunk), chunk)

    def remote(src, dst, send, recv, device):
        return pltpu.make_async_remote_copy(
            src_ref=src, dst_ref=dst, send_sem=send, recv_sem=recv,
            device_id=device, device_id_type=MESH,
        )

    def grad_copy(c):
        source = pl.ds(pl.multiple_of(nf * depth + c * chunk, chunk), chunk)
        return remote(
            grad_hbm.at[0, :, source, :], peer_grad.at[:, rows(c), :],
            grad_send.at[c], grad_recv.at[c], partner,
        )

    def x_move(z, th, side):
        return remote(
            xbuf.at[z, th], xbuf.at[z, th], x_send.at[side, z, th], x_recv.at[z, th],
            up if side == 1 else down,
        )

    def x_own(side):
        return remote(
            x_hbm.at[:, :, half(f)], xbuf.at[t, f], x_send.at[side, t, f], x_recv.at[t, f],
            up if side == 1 else down,
        )

    x_swap = remote(x_hbm.at[:, :, half(nf)], xbuf.at[t, f], x_swap_send.at[0], x_recv.at[t, f], partner)

    def both_ways(act):
        @pl.when(t < n_tp - 1)
        def _():
            act(1)

        @pl.when(t > 0)
        def _():
            act(0)

    grad_copy(0).start()
    x_swap.start()
    both_ways(lambda side: x_own(side).start())
    for c in range(1, W_CHUNKS):
        grad_copy(c).start()

    def w_copy(c, way):
        return remote(
            wbuf.at[r, :, rows(c), :], wbuf.at[r, :, rows(c), :],
            w_send.at[way, c], w_recv.at[r, c], dev_x if way == 0 else dev_y,
        )

    def w_arrived(owner, c):
        remote(
            wbuf.at[owner, :, rows(c), :], wbuf.at[owner, :, rows(c), :],
            w_send.at[0, c], w_recv.at[owner, c], dev_x,
        ).wait_recv()

    def w_forward(c):
        owner, device = (rx, dev_y) if c % 2 == 0 else (ry, dev_x)
        return remote(
            wbuf.at[owner, :, rows(c), :], wbuf.at[owner, :, rows(c), :],
            w_fwd_send.at[c], w_recv.at[owner, c], device,
        )

    def x_arrived(z, th):
        x_move(z, th, 1).wait_recv()

    for copy in local[:4]:
        copy.wait()

    first_bias = 1.0 - 0.9**10
    second_bias = 1.0 - 0.95**10

    def adam(c):
        def sub(i, carry):
            at = pl.ds(pl.multiple_of(c * chunk + i * ADAM_SUB, ADAM_SUB), ADAM_SUB)
            gradient = own_grad[:, at, :].astype(jnp.float32) + peer_grad[:, at, :].astype(jnp.float32)
            new_one = 0.9 * one[:, at, :] + (1.0 - 0.9) * gradient
            new_two = 0.95 * two[:, at, :] + (1.0 - 0.95) * gradient * gradient
            update = new_one / first_bias / (jnp.sqrt(new_two / second_bias) + 1e-08)
            old = master[:, at, :]
            new_master = old - 0.001 * (update + 0.1 * old)
            one[:, at, :] = new_one
            two[:, at, :] = new_two
            master[:, at, :] = new_master
            wbuf[r, :, at, :] = new_master.astype(jnp.bfloat16)
            return carry

        lax.fori_loop(0, chunk // ADAM_SUB, sub, 0)

    for c in range(W_CHUNKS):
        grad_copy(c).wait_recv()
        adam(c)
        if c == 0:
            x_arrived(t, nf)
            both_ways(lambda side: x_move(t, nf, side).start())
        else:
            w_copy(c - 1, 0).start()
            w_copy(c - 1, 1).start()
    outs = [
        pltpu.make_async_copy(master, master_out, out_sem.at[0]),
        pltpu.make_async_copy(one, one_out, out_sem.at[1]),
        pltpu.make_async_copy(two, two_out, out_sem.at[2]),
    ]
    for copy in outs:
        copy.start()
    w_copy(W_CHUNKS - 1, 0).start()
    w_copy(W_CHUNKS - 1, 1).start()
    local[4].wait()
    local[5].wait()

    ends_up, ends_down = t + 1 == n_tp - 1, t == 1

    def x_wait(k, th):
        @pl.when(t - k >= 0)
        def _():
            x_arrived(t - k, th)

        @pl.when(t + k < n_tp)
        def _():
            x_arrived(t + k, th)

    def x_forward(k, th, go_up, go_down):
        @pl.when((t - k >= 0) & (t < n_tp - 1) & go_up)
        def _():
            x_move(t - k, th, 1).start()

        @pl.when((t + k < n_tp) & (t > 0) & go_down)
        def _():
            x_move(t + k, th, 0).start()

    def x_first_half():
        x_wait(1, f)
        x_forward(1, f, ends_up, ends_down)

    def x_second_half():
        x_wait(1, nf)
        x_forward(1, nf, True, True)
        x_forward(1, f, jnp.logical_not(ends_up), jnp.logical_not(ends_down))

    def x_far(k, th):
        x_wait(k, th)
        x_forward(k, th, True, True)

    def w_step(c):
        w_arrived(rx, c)
        w_arrived(ry, c)
        w_forward(c).start()

    kv_rows, cache_len = kv_raw.shape[:2]
    pieces = kv_rows // 8

    def split_cache(quarter):
        def body(i, carry):
            row = (quarter * pieces + i) * 2
            at = pl.ds(pl.multiple_of(row * cache_len, 2 * cache_len), 2 * cache_len)
            for j in range(2):
                kv_flat[j, at, :] = kv_raw[pl.ds(row, 2), :, j, :].reshape(2 * cache_len, -1)
            return carry

        lax.fori_loop(0, pieces, body, 0)

    split_cache(0)
    x_first_half()
    split_cache(1)
    w_step(0)
    split_cache(2)
    x_second_half()
    split_cache(3)
    cached_copy = pltpu.make_async_copy(kv_flat, cached_out, out_sem.at[3])
    cached_copy.start()
    w_step(1)
    w_step(2)
    x_far(2, nf)
    w_step(3)
    x_far(2, f)

    acc[...] = jnp.zeros_like(acc)

    x_rows = xbuf.shape[2]
    x_part = x_rows // 4
    flat_part = xflat.shape[0] // 4

    def multiply(z, th):
        def flatten(i, carry):
            at = pl.ds(pl.multiple_of(i * flat_part, flat_part), flat_part)
            xflat[at, :] = xbuf[z, th, pl.ds(i * x_part, x_part)].reshape(flat_part, depth)
            return carry

        lax.fori_loop(0, 4, flatten, 0, unroll=True)

        def one_side(kv, carry):
            acc[th, kv] += jnp.dot(xflat[...], wbuf[z, kv], preferred_element_type=jnp.float32)
            return carry

        lax.fori_loop(0, 2, one_side, 0, unroll=True)

    for c in range(W_CHUNKS):
        w_arrived(rd, c)

    def step(j, carry):
        k = j // 2
        th = nf + lax.rem(j, 2) * (1 - 2 * nf)

        def side(s, inner):
            z = t + (2 * s - 1) * k

            @pl.when((z >= 0) & (z < n_tp))
            def _():
                @pl.when(k == n_tp - 1)
                def _():
                    x_arrived(z, th)

                multiply(z, th)

            return inner

        lax.fori_loop(jnp.where(k == 0, 1, 0), 2, side, 0)
        return carry

    lax.fori_loop(0, 2 * n_tp - 1, step, 0)

    swap = remote(acc.at[nf], partner_acc, acc_send.at[0], acc_recv.at[0], partner)
    swap.start()
    step(2 * n_tp - 1, 0)
    for c in range(W_CHUNKS):
        grad_copy(c).wait_send()
        w_copy(c, 0).wait_send()
        w_copy(c, 1).wait_send()
        w_forward(c).wait_send()
    x_swap.wait_send()
    both_ways(lambda side: x_own(side).wait_send())
    both_ways(lambda side: x_move(t, nf, side).wait_send())
    for k in range(1, n_tp - 1):
        for th in (f, nf):
            @pl.when((t - k >= 0) & (t < n_tp - 1))
            def _():
                x_move(t - k, th, 1).wait_send()

            @pl.when((t + k < n_tp) & (t > 0))
            def _():
                x_move(t + k, th, 0).wait_send()
    for copy in outs:
        copy.wait()
    cached_copy.wait()
    swap.wait_recv()
    fresh_out[...] = (acc[f] + partner_acc[...]).astype(jnp.bfloat16)
    swap.wait_send()


def tail_kernel(
    lengths, q_ref, kv_ref, fresh_in, master_in, one_in, two_in,
    context, master_out, one_out, two_out, fresh_ref, sem,
):
    block = pl.program_id(0)
    moves = [
        pltpu.make_async_copy(master_in, master_out, sem.at[1]),
        pltpu.make_async_copy(one_in, one_out, sem.at[2]),
        pltpu.make_async_copy(two_in, two_out, sem.at[3]),
    ]

    @pl.when(block == 0)
    def _():
        fresh_copy = pltpu.make_async_copy(fresh_in, fresh_ref, sem.at[0])
        fresh_copy.start()
        for move in moves:
            move.start()
        fresh_copy.wait()

    step_rows, step_count, features = q_ref.shape
    row_count = TAIL_ROWS
    head = HD
    cache_len = kv_ref.shape[1] // step_rows
    cached = row_count * cache_len
    tokens = row_count * step_count
    keys = cached + tokens
    groups = fresh_ref.shape[2] // head
    per_group = features // head // groups
    column = lax.broadcasted_iota(jnp.int32, (1, keys), 1)
    is_old = column < cached
    new_column = column - cached
    key_row = jnp.where(is_old, column // cache_len, new_column // step_count)
    position = column - key_row * cache_len
    new_row = jnp.where(is_old, -1, key_row)
    token = lax.broadcasted_iota(jnp.int32, (tokens, 1), 0)
    row = token // step_count
    new_valid = (new_row == row) & (new_column <= token)
    low = -0.7 * float(jnp.finfo(jnp.float32).max)
    factor = head**-0.5 * LOG2E
    contract = (((1,), (1,)), ((), ()))
    for part in range(step_rows // row_count):
        first_row = part * row_count
        start = block * step_rows + first_row
        limit = jnp.zeros((1, keys), jnp.int32)
        for at in range(row_count):
            limit = jnp.where(key_row == at, lengths[start + at], limit)
        valid = (jnp.where(is_old & (position < limit), key_row, -1) == row) | new_valid
        here = pl.ds(pl.multiple_of(start * step_count, tokens), tokens)
        old = slice(first_row * cache_len, first_row * cache_len + cached)
        mine = slice(first_row, first_row + row_count)
        for group in range(groups):
            cols = slice(group * head, (group + 1) * head)
            query = jnp.concatenate(
                [
                    q_ref[mine, :, (group * per_group + h) * head : (group * per_group + h + 1) * head].reshape(
                        tokens, head
                    )
                    for h in range(per_group)
                ],
                axis=0,
            )
            key = jnp.concatenate([kv_ref[0, old, cols], fresh_ref[0, here, cols]], axis=0)
            value = jnp.concatenate([kv_ref[1, old, cols], fresh_ref[1, here, cols]], axis=0)
            scores = lax.dot_general(query, key, contract, preferred_element_type=jnp.float32)
            scores = jnp.where(valid[None], scores.reshape(per_group, tokens, keys), low)
            weights = jnp.exp2((scores - jnp.max(scores, axis=-1, keepdims=True)) * factor)
            weights = weights * (1.0 / jnp.sum(weights, axis=-1, keepdims=True))
            weights = weights.astype(jnp.bfloat16).reshape(per_group * tokens, keys)
            out = jnp.dot(weights, value, preferred_element_type=jnp.float32)
            for h in range(per_group):
                at = (group * per_group + h) * head
                piece = out[h * tokens : (h + 1) * tokens].reshape(row_count, step_count, head)
                context[mine, :, at : at + head] = piece.astype(jnp.bfloat16)

    @pl.when(block == pl.num_programs(0) - 1)
    def _():
        for move in moves:
            move.wait()


def fused_device(n_rep, grad_parts, master_weight, moment_one, moment_two, layer_inputs, queries, kv_cache, lengths):
    row_count, step_count, features = layer_inputs.shape
    _, depth, width = master_weight.shape
    n_tp = n_rep
    tokens = row_count * step_count
    cache_len = kv_cache.shape[1]
    bf16, f32 = jnp.bfloat16, jnp.float32
    dma = pltpu.SemaphoreType.DMA
    state = jax.ShapeDtypeStruct(master_weight.shape, f32)
    any_spec = pl.BlockSpec(memory_space=pl.ANY)
    hbm_spec = pl.BlockSpec(memory_space=pltpu.HBM)
    in_place = [
        pltpu.with_memory_space_constraint(array, pltpu.HBM)
        for array in (grad_parts, master_weight, moment_one, moment_two, layer_inputs, kv_cache)
    ]
    fresh, cached, master, one, two = pl.pallas_call(
        functools.partial(learner_kernel, (n_tp, depth)),
        out_shape=(
            jax.ShapeDtypeStruct((2, tokens, width), bf16),
            jax.ShapeDtypeStruct((2, row_count * cache_len, width), bf16),
            state,
            state,
            state,
        ),
        in_specs=[hbm_spec] * 6,
        out_specs=(pl.BlockSpec(memory_space=pltpu.VMEM), hbm_spec, any_spec, any_spec, any_spec),
        scratch_shapes=[
            pltpu.VMEM((2, depth, width), bf16),
            pltpu.VMEM((2, depth, width), bf16),
            pltpu.VMEM((2, depth, width), f32),
            pltpu.VMEM((2, depth, width), f32),
            pltpu.VMEM((2, depth, width), f32),
            pltpu.VMEM((n_rep, 2, depth, width), bf16),
            pltpu.VMEM((n_tp, 2, row_count, step_count, depth), bf16),
            pltpu.VMEM((tokens, depth), bf16),
            pltpu.VMEM((2, 2, tokens, width), f32),
            pltpu.VMEM((2, tokens, width), f32),
            pltpu.VMEM(kv_cache.shape, bf16),
            pltpu.VMEM((2, row_count * cache_len, width), bf16),
            dma((6,)),
            dma((4,)),
            dma((W_CHUNKS,)),
            dma((W_CHUNKS,)),
            dma((2, n_tp, 2)),
            dma((n_tp, 2)),
            dma((1,)),
            dma((2, W_CHUNKS)),
            dma((n_rep, W_CHUNKS)),
            dma((W_CHUNKS,)),
            dma((1,)),
            dma((1,)),
        ],
        compiler_params=pltpu.CompilerParams(
            collective_id=0, has_side_effects=True, vmem_limit_bytes=36 * 1024 * 1024
        ),
    )(*in_place)
    step_rows = TAIL_ROWS * TAIL_BLOCKS
    token_spec = pl.BlockSpec((step_rows, step_count, features), lambda i, *_: (i, 0, 0))
    context, master, one, two = pl.pallas_call(
        tail_kernel,
        out_shape=(jax.ShapeDtypeStruct(queries.shape, bf16), state, state, state),
        grid_spec=pltpu.PrefetchScalarGridSpec(
            num_scalar_prefetch=1,
            grid=(row_count // step_rows,),
            in_specs=[
                token_spec,
                pl.BlockSpec((2, step_rows * cache_len, width), lambda i, *_: (0, i, 0)),
                any_spec,
                any_spec,
                any_spec,
                any_spec,
            ],
            out_specs=(token_spec, hbm_spec, hbm_spec, hbm_spec),
            scratch_shapes=[pltpu.VMEM((2, tokens, width), bf16), dma((4,))],
        ),
        compiler_params=pltpu.CompilerParams(
            dimension_semantics=("arbitrary",), vmem_limit_bytes=16 * 1024 * 1024
        ),
    )(lengths, queries, cached, fresh, master, one, two)
    return (master, one, two, context)


beta_one = 0.9
beta_two = 0.95
learning_rate = 0.001
weight_decay = 0.1
epsilon = 1e-08
first_bias = 1.0 - 0.9**10
second_bias = 1.0 - 0.95**10


def adamw_update(gradient, master, moment_one, moment_two):
    new_one = beta_one * moment_one + (1.0 - beta_one) * gradient
    new_two = beta_two * moment_two + (1.0 - beta_two) * gradient * gradient
    update = new_one / first_bias / (jnp.sqrt(new_two / second_bias) + epsilon)
    new_master = master - learning_rate * (update + weight_decay * master)
    return (new_one, new_two, new_master)


def attend(queries, kv_cache, fresh_keys, fresh_values, lengths):
    row_count = queries.shape[0]
    step_count = queries.shape[1]
    kv_heads = fresh_keys.shape[2]
    cache_len = kv_cache.shape[1]
    grouped = queries.reshape(row_count, step_count, kv_heads, -1, HD)
    cached_keys = kv_cache[:, :, 0].reshape(row_count, cache_len, kv_heads, HD)
    cached_values = kv_cache[:, :, 1].reshape(row_count, cache_len, kv_heads, HD)
    scaling = 1.0 / jnp.sqrt(jnp.float32(HD))
    cached_scores = (
        jnp.einsum("rsgqd,rcgd->rsgqc", grouped, cached_keys, preferred_element_type=jnp.float32)
        * scaling
    )
    fresh_scores = (
        jnp.einsum("rsgqd,rugd->rsgqu", grouped, fresh_keys, preferred_element_type=jnp.float32)
        * scaling
    )
    valid_old = jnp.arange(cache_len, dtype=jnp.int32)[None, :] < lengths[:, None]
    valid_old = valid_old[:, None, None, None, :]
    steps_index = jnp.arange(step_count, dtype=jnp.int32)
    valid_new = (steps_index[None, :] <= steps_index[:, None])[None, :, None, None, :]
    scores = jnp.concatenate(
        [
            jnp.where(valid_old, cached_scores, -jnp.inf),
            jnp.where(valid_new, fresh_scores, -jnp.inf),
        ],
        axis=-1,
    )
    row_max = jnp.max(scores, axis=-1, keepdims=True)
    exponent = jnp.exp(scores - row_max)
    weights = (exponent / jnp.sum(exponent, axis=-1, keepdims=True)).astype(jnp.bfloat16)
    output = jnp.einsum(
        "rsgqc,rcgd->rsgqd",
        weights[..., :cache_len],
        cached_values,
        preferred_element_type=jnp.float32,
    )
    output = output + jnp.einsum(
        "rsgqu,rugd->rsgqd",
        weights[..., cache_len:],
        fresh_values,
        preferred_element_type=jnp.float32,
    )
    return output.astype(jnp.bfloat16).reshape(row_count, step_count, -1)


def on_device(
    grad_parts, master_weight, moment_one, moment_two, layer_inputs, queries, kv_cache, lengths
):
    gradient = lax.psum_scatter(
        grad_parts[0].astype(jnp.float32).astype(jnp.bfloat16),
        "fsdp",
        scatter_dimension=1,
        tiled=True,
    ).astype(jnp.float32)
    new_one, new_two, new_master = adamw_update(gradient, master_weight, moment_one, moment_two)
    rollout_weight = new_master.astype(jnp.bfloat16)
    row_count = layer_inputs.shape[0]
    step_count = layer_inputs.shape[1]
    gathered = lax.all_gather(layer_inputs, "tp", axis=2, tiled=True)
    flattened = gathered.reshape(row_count * step_count, gathered.shape[2])
    projected = jnp.einsum(
        "td,kdc->ktc",
        flattened,
        lax.all_gather(rollout_weight, ("rep", "fsdp"), axis=1, tiled=True),
        preferred_element_type=jnp.float32,
    )
    fresh_pair = projected.astype(jnp.bfloat16).reshape(2, row_count, step_count, -1, HD)
    context = attend(queries, kv_cache, fresh_pair[0], fresh_pair[1], lengths)
    return (new_master, new_one, new_two, context)


def solution(mesh):
    shape = mesh.shape
    fits = shape["rep"] == 4 and shape["tp"] == 4 and shape["fsdp"] == 2
    run = functools.partial(fused_device, shape["rep"]) if fits else on_device
    return jax.shard_map(
        run,
        mesh=mesh,
        in_specs=(
            P("fsdp", None, "rep", "tp"),
            P(None, ("rep", "fsdp"), "tp"),
            P(None, ("rep", "fsdp"), "tp"),
            P(None, ("rep", "fsdp"), "tp"),
            P(("rep", "fsdp"), None, "tp"),
            P(("rep", "fsdp"), None, "tp"),
            P(("rep", "fsdp"), None, None, "tp"),
            P(("rep", "fsdp")),
        ),
        out_specs=(
            P(None, ("rep", "fsdp"), "tp"),
            P(None, ("rep", "fsdp"), "tp"),
            P(None, ("rep", "fsdp"), "tp"),
            P(("rep", "fsdp"), None, "tp"),
        ),
        check_vma=False,
    )
```
